32 devices in a mesh: row: 4 (over y, x), col: 8 (over z, core).
Axes of the slice: x: 2, y: 2, z: 4, core: 2. Of those that a mesh axis runs over, the one named last changes fastest.
Arguments:
- pointmaps: bfloat16 [64, 64, 2, 3, 14336], P('row', 'col'), may hold values from -6 to 6
- confidence: bfloat16 [64, 64, 2, 14336], P('row', 'col'), may hold values from 1 to 10
- valid_blocks: int32 [64, 64, 64], P('row', 'col'), may hold values 0 or 1
- log_depth: float32 [64, 14336], P('row', 'col'), may hold values from 0 to 1.4
- camera: float32 [64, 8], replicated, may hold values from -1 to 5.8, as said below
- pair_pose: float32 [64, 64, 8], P('row', 'col'), may hold values from -1 to 1.2, as said below
- step_sizes: float32 [3], replicated, may hold values from 0.02 to 0.2
Outputs:
- new_log_depth: float32 [64, 14336], P('row', 'col')
- new_camera: float32 [64, 8], replicated
- new_pair_pose: float32 [64, 64, 8], P('row', 'col')
The draws below stay inside these ranges and needn't reach their ends.
Inputs may be any that keep to these rules, and one draw needn't show every extreme that they name: `camera`: columns 0 to 3 hold a quaternion whose first entry lies in 0.8 to 1.2 and the others in -0.3 to 0.3; columns 4 to 6 a translation in -1 to 1; column 7 a log focal length in pixels, 5.2 to 5.8. `pair_pose`: columns 0 to 3 hold a quaternion whose first entry lies in 0.8 to 1.2 and the others in -0.3 to 0.3; columns 4 to 6 a translation in -1 to 1; column 7 a log scale in -0.5 to 0.5.
All inputs are finite; a program needn't handle non-finite values. No bound on the sum of `valid_blocks` on one device may be relied on, other than what follows from the above.
Results may differ from the reference program's by a relative error of at most 0.00055.
Values sent between devices are 32-bit elements; how exact they have to be, the bound alone decides.
No kernel may reach another device: no remote copies, remote signals or barrier semaphores. Data moves between devices by JAX's collectives and lax.ppermute only.
A program may use at most 192 MiB of HBM per device.

```python
import math
import jax
import jax.numpy as jnp
from jax import lax

IMAGES = 64
IMG_WIDTH = 224
IMG_HEIGHT = 224
WIN_ROWS = 64
ADAM_STEPS = 2
PIXELS = 14336


def draw_camera(key, part):
    key = jax.random.fold_in(key, 11)
    keys = jax.random.split(key, 4)
    leading = jax.random.uniform(keys[0], (IMAGES, 1), jnp.float32, 0.8, 1.2)
    others = jax.random.uniform(keys[1], (IMAGES, 3), jnp.float32, -0.3, 0.3)
    shift = jax.random.uniform(keys[2], (IMAGES, 3), jnp.float32, -1.0, 1.0)
    focal_log = jax.random.uniform(keys[3], (IMAGES, 1), jnp.float32, 5.2, 5.8)
    return jnp.concatenate([leading, others, shift, focal_log], axis=1)


def draw_pair_pose(key, part):
    key = jax.random.fold_in(key, 23)
    keys = jax.random.split(key, 4)
    leading = jax.random.uniform(keys[0], (IMAGES, IMAGES, 1), jnp.float32, 0.8, 1.2)
    others = jax.random.uniform(keys[1], (IMAGES, IMAGES, 3), jnp.float32, -0.3, 0.3)
    shift = jax.random.uniform(keys[2], (IMAGES, IMAGES, 3), jnp.float32, -1.0, 1.0)
    scale_log = jax.random.uniform(keys[3], (IMAGES, IMAGES, 1), jnp.float32, -0.5, 0.5)
    return jnp.concatenate([leading, others, shift, scale_log], axis=2)


def touch_ends(drawn, rng, smallest, largest):
    longest = drawn.shape.index(max(drawn.shape))
    spots = []
    for shift in (0, 1):
        where = [jax.random.randint(jax.random.fold_in(rng, axis), (), 0, length) for axis, length in enumerate(drawn.shape)]
        where[longest] = (where[longest] + shift) % drawn.shape[longest]
        spots.append(tuple(where))
    return drawn.at[spots[0]].set(smallest).at[spots[1]].set(largest)


def block_scale(stream_key, shape, cuts, low, top_value):
    def one(dim, shards_of):
        draws = jax.random.uniform(jax.random.fold_in(jax.random.fold_in(stream_key, 6), dim), (shards_of,), jnp.float32, low / len(cuts), top_value / len(cuts))
        return jnp.repeat(jnp.exp(draws), shape[dim] // shards_of).reshape((-1,) + (1,) * (len(shape) - dim - 1))

    gain = one(*cuts[0])
    for cut in cuts[1:]:
        gain = gain * one(*cut)
    return gain


def bell_draw(own_key, dims, spread, bound, shards=(), held_as=jnp.bfloat16):
    entries = spread * jax.random.normal(own_key, dims, jnp.float32)
    if shards:
        entries = entries * block_scale(own_key, dims, shards, -0.22, 0.18)
    return jnp.clip(entries, -bound, bound).astype(held_as)


def setup_inputs(seed: int = 0) -> dict:
    key_of = jax.random.split(jax.random.key(seed), 8)
    pointmaps = bell_draw(key_of[0], (IMAGES, IMAGES, 2, 3, PIXELS), 1.0, 6.0, ((0, 4), (1, 8)))
    confidence = jnp.clip(jnp.exp(math.log(10.0) - 2.3025851 * jax.random.uniform(key_of[1], (IMAGES, IMAGES, 2, PIXELS), jnp.float32) ** block_scale(key_of[1], (IMAGES, IMAGES, 2, PIXELS), ((0, 4), (1, 8)), -0.2, 0.2)), 1.0, 10.0).astype(jnp.bfloat16)
    valid_blocks = touch_ends((jax.random.randint(key_of[2], (IMAGES, IMAGES, WIN_ROWS), 0, 4) < 3).astype(jnp.int32), jax.random.fold_in(key_of[2], 1), 0, 1)
    log_depth = jnp.clip(1.4 * jax.random.uniform(key_of[3], (IMAGES, PIXELS), jnp.float32) ** block_scale(key_of[3], (IMAGES, PIXELS), ((0, 4), (1, 8)), -0.2, 0.2), 0.0, 1.4)
    camera = draw_camera(jax.random.fold_in(key_of[7], 71), 0)
    pair_pose = draw_pair_pose(jax.random.fold_in(key_of[7], 71), 0)
    step_sizes = jnp.clip(jax.random.uniform(key_of[6], (3,), jnp.float32, 0.02, 0.2), 0.02, 0.2)
    return dict(pointmaps=pointmaps, confidence=confidence, valid_blocks=valid_blocks, log_depth=log_depth, camera=camera, pair_pose=pair_pose, step_sizes=step_sizes)


BETA_ONE = 0.9
BETA_TWO = 0.999
ADAM_EPS = 0.001
SOFTEN = 0.01

def rotation(quaternion):
    length = jnp.sqrt(lax.optimization_barrier(jnp.sum(quaternion * quaternion, axis=-1)))
    w = quaternion[..., 0] / length
    x = quaternion[..., 1] / length
    y = quaternion[..., 2] / length
    z = quaternion[..., 3] / length
    return [[1.0 - 2.0 * (y * y + z * z), 2.0 * (x * y - w * z), 2.0 * (x * z + w * y)], [2.0 * (x * y + w * z), 1.0 - 2.0 * (x * x + z * z), 2.0 * (y * z - w * x)], [2.0 * (x * z - w * y), 2.0 * (y * z + w * x), 1.0 - 2.0 * (x * x + y * y)]]

def world_points(log_depths, cameras):
    pixel_count = log_depths.shape[-1]
    position = jnp.arange(pixel_count, dtype=jnp.int32)
    across = (position % IMG_WIDTH).astype(jnp.float32) - (IMG_WIDTH - 1) / 2.0
    downward = (position // IMG_WIDTH + (IMG_HEIGHT - WIN_ROWS) // 2).astype(jnp.float32) - (IMG_HEIGHT - 1) / 2.0
    focal_len = jnp.exp(cameras[:, 7:8])
    depth_map = jnp.exp(log_depths)
    ray_parts = (across[None, :] / focal_len * depth_map, downward[None, :] / focal_len * depth_map, depth_map)
    turned = rotation(cameras[:, 0:4])
    return [turned[k][0][:, None] * ray_parts[0] + turned[k][1][:, None] * ray_parts[1] + turned[k][2][:, None] * ray_parts[2] + cameras[:, 4 + k][:, None] for k in range(3)]

def pair_loss(first_depth, second_depth, first_camera, second_camera, pair_params, pointmaps, confidence, valid_blocks, first_ids, second_ids):
    first_world = world_points(first_depth, first_camera)
    second_world = world_points(second_depth, second_camera)
    pair_rotation = rotation(pair_params[..., 0:4])
    pair_scale = jnp.exp(pair_params[..., 7])
    pair_keep = (first_ids[:, None] != second_ids[None, :]).astype(jnp.float32)
    pixel_keep = jnp.repeat(valid_blocks.astype(jnp.float32), IMG_WIDTH, axis=2) * pair_keep[:, :, None]
    loss_sum = jnp.zeros((), jnp.float32)
    for side_index in range(2):
        if side_index == 0:
            points_side = [first_world[k][:, None, :] for k in range(3)]
        else:
            points_side = [second_world[k][None, :, :] for k in range(3)]
        source = [pointmaps[:, :, side_index, k, :].astype(jnp.float32) for k in range(3)]
        squared = SOFTEN
        for k in range(3):
            aligned = pair_scale[..., None] * (pair_rotation[k][0][..., None] * source[0] + pair_rotation[k][1][..., None] * source[1] + pair_rotation[k][2][..., None] * source[2]) + pair_params[..., 4 + k][..., None]
            residual = points_side[k] - aligned
            squared = squared + residual * residual
        weight = confidence[:, :, side_index, :].astype(jnp.float32) * pixel_keep
        loss_sum = loss_sum + jnp.sum(weight * jnp.sqrt(squared))
    return loss_sum / (2.0 * (IMAGES - 1))

def adam_step(param, grad, first, second, step_number, step_size):
    first = BETA_ONE * first + (1.0 - BETA_ONE) * grad
    second = BETA_TWO * second + (1.0 - BETA_TWO) * grad * grad
    update = step_size * (first / (1.0 - BETA_ONE ** step_number)) / (jnp.sqrt(second / (1.0 - BETA_TWO ** step_number)) + ADAM_EPS)
    return (param - update, first, second)

def reference(pointmaps, confidence, valid_blocks, log_depth, camera, pair_pose, step_sizes):
    image_ids = jnp.arange(IMAGES, dtype=jnp.int32)

    def total_loss(log_depths, cameras, pair_params):

        def one_row(image_index):
            first_depth = lax.dynamic_slice_in_dim(log_depths, image_index, 1, 0)
            first_camera = lax.dynamic_slice_in_dim(cameras, image_index, 1, 0)
            row_params = lax.dynamic_slice_in_dim(pair_params, image_index, 1, 0)
            row_points = lax.dynamic_slice_in_dim(pointmaps, image_index, 1, 0)
            row_confidence = lax.dynamic_slice_in_dim(confidence, image_index, 1, 0)
            row_valid = lax.dynamic_slice_in_dim(valid_blocks, image_index, 1, 0)
            return pair_loss(first_depth, log_depths, first_camera, cameras, row_params, row_points, row_confidence, row_valid, image_index[None], image_ids)
        return jnp.sum(lax.map(jax.checkpoint(one_row), image_ids))
    depth_now, camera_now, pair_now = (log_depth, camera, pair_pose)
    depth_first = jnp.zeros_like(log_depth)
    depth_second = jnp.zeros_like(log_depth)
    camera_first = jnp.zeros_like(camera)
    camera_second = jnp.zeros_like(camera)
    pair_first = jnp.zeros_like(pair_pose)
    pair_second = jnp.zeros_like(pair_pose)
    for step_number in range(1, ADAM_STEPS + 1):
        gradients = jax.grad(total_loss, argnums=(0, 1, 2))(depth_now, camera_now, pair_now)
        depth_now, depth_first, depth_second = adam_step(depth_now, gradients[0], depth_first, depth_second, step_number, step_sizes[0])
        camera_now, camera_first, camera_second = adam_step(camera_now, gradients[1], camera_first, camera_second, step_number, step_sizes[1])
        pair_now, pair_first, pair_second = adam_step(pair_now, gradients[2], pair_first, pair_second, step_number, step_sizes[2])
    return (depth_now, camera_now, pair_now)
```

```python
import functools

import numpy as np

import jax
import jax.numpy as jnp
from jax import lax
from jax.experimental import pallas as pl
from jax.experimental.pallas import tpu as pltpu
from jax.sharding import PartitionSpec as P

IMAGES = 64
IMG_WIDTH = 224
IMG_HEIGHT = 224
WIN_ROWS = 64
ADAM_STEPS = 2

BETA_ONE = 0.9
BETA_TWO = 0.999
ADAM_EPS = 0.001
SOFTEN = 0.01

LANES = 128
SUBLANES = 8
TABLE_PAIRS = 64


def rotation(quaternion):
    length = jnp.sqrt(jnp.sum(quaternion * quaternion, axis=-1))
    w = quaternion[..., 0] / length
    x = quaternion[..., 1] / length
    y = quaternion[..., 2] / length
    z = quaternion[..., 3] / length
    return [
        [1.0 - 2.0 * (y * y + z * z), 2.0 * (x * y - w * z), 2.0 * (x * z + w * y)],
        [2.0 * (x * y + w * z), 1.0 - 2.0 * (x * x + z * z), 2.0 * (y * z - w * x)],
        [2.0 * (x * z - w * y), 2.0 * (y * z + w * x), 1.0 - 2.0 * (x * x + y * y)],
    ]


def adam_step(param, grad, first, second, step_number, step_size):
    first = BETA_ONE * first + (1.0 - BETA_ONE) * grad
    second = BETA_TWO * second + (1.0 - BETA_TWO) * grad * grad
    update = (
        step_size
        * (first / (1.0 - BETA_ONE**step_number))
        / (jnp.sqrt(second / (1.0 - BETA_TWO**step_number)) + ADAM_EPS)
    )
    return (param - update, first, second)


def world_points(log_depths, cameras):
    pixel_count = log_depths.shape[-1]
    position = jnp.arange(pixel_count, dtype=jnp.int32)
    across = (position % IMG_WIDTH).astype(jnp.float32) - (IMG_WIDTH - 1) / 2.0
    downward = (position // IMG_WIDTH + (IMG_HEIGHT - WIN_ROWS) // 2).astype(jnp.float32) - (
        IMG_HEIGHT - 1
    ) / 2.0
    focal_len = jnp.exp(cameras[:, 7:8])
    depth_map = jnp.exp(log_depths)
    ray_parts = (
        across[None, :] / focal_len * depth_map,
        downward[None, :] / focal_len * depth_map,
        depth_map,
    )
    turned = rotation(cameras[:, 0:4])
    return [
        turned[k][0][:, None] * ray_parts[0]
        + turned[k][1][:, None] * ray_parts[1]
        + turned[k][2][:, None] * ray_parts[2]
        + cameras[:, 4 + k][:, None]
        for k in range(3)
    ]


def pair_loss(
    first_depth,
    second_depth,
    first_camera,
    second_camera,
    pair_params,
    pointmaps,
    confidence,
    valid_blocks,
    first_ids,
    second_ids,
):
    first_world = world_points(first_depth, first_camera)
    second_world = world_points(second_depth, second_camera)
    pair_rotation = rotation(pair_params[..., 0:4])
    pair_scale = jnp.exp(pair_params[..., 7])
    pair_keep = (first_ids[:, None] != second_ids[None, :]).astype(jnp.float32)
    pixel_keep = (
        jnp.repeat(valid_blocks.astype(jnp.float32), IMG_WIDTH, axis=2) * pair_keep[:, :, None]
    )
    loss_sum = jnp.zeros((), jnp.float32)
    for side_index in range(2):
        if side_index == 0:
            points_side = [first_world[k][:, None, :] for k in range(3)]
        else:
            points_side = [second_world[k][None, :, :] for k in range(3)]
        source = [pointmaps[:, :, side_index, k, :].astype(jnp.float32) for k in range(3)]
        squared = SOFTEN
        for k in range(3):
            aligned = (
                pair_scale[..., None]
                * (
                    pair_rotation[k][0][..., None] * source[0]
                    + pair_rotation[k][1][..., None] * source[1]
                    + pair_rotation[k][2][..., None] * source[2]
                )
                + pair_params[..., 4 + k][..., None]
            )
            residual = points_side[k] - aligned
            squared = squared + residual * residual
        weight = confidence[:, :, side_index, :].astype(jnp.float32) * pixel_keep
        loss_sum = loss_sum + jnp.sum(weight * jnp.sqrt(squared))
    return loss_sum / (2.0 * (IMAGES - 1))


def general_body(pointmaps, confidence, valid_blocks, log_depth, camera, pair_pose, step_sizes):
    row_count = pointmaps.shape[0]
    col_count = pointmaps.shape[1]
    row_index = lax.axis_index("row")
    col_index = lax.axis_index("col")
    first_ids = row_index * row_count + jnp.arange(row_count, dtype=jnp.int32)
    second_ids = col_index * col_count + jnp.arange(col_count, dtype=jnp.int32)

    def local_loss(row_depth, col_depth, cameras, pair_params):
        first_camera = lax.dynamic_slice_in_dim(cameras, row_index * row_count, row_count, 0)
        second_camera = lax.dynamic_slice_in_dim(cameras, col_index * col_count, col_count, 0)
        return pair_loss(
            row_depth,
            col_depth,
            first_camera,
            second_camera,
            pair_params,
            pointmaps,
            confidence,
            valid_blocks,
            first_ids,
            second_ids,
        )

    depth_now, camera_now, pair_now = (log_depth, camera, pair_pose)
    depth_first = jnp.zeros_like(log_depth)
    depth_second = jnp.zeros_like(log_depth)
    camera_first = jnp.zeros_like(camera)
    camera_second = jnp.zeros_like(camera)
    pair_first = jnp.zeros_like(pair_pose)
    pair_second = jnp.zeros_like(pair_pose)
    for step_number in range(1, ADAM_STEPS + 1):
        row_depth = lax.all_gather(depth_now, "col", axis=1, tiled=True)
        every_image = lax.all_gather(depth_now, "row", axis=0, tiled=True)
        col_depth = lax.all_to_all(every_image, "col", split_axis=0, concat_axis=1, tiled=True)
        row_grad, col_grad, cam_grad, pair_grad = jax.grad(local_loss, argnums=(0, 1, 2, 3))(
            row_depth, col_depth, camera_now, pair_now
        )
        returned = lax.all_to_all(col_grad, "col", split_axis=1, concat_axis=0, tiled=True)
        from_cols = lax.psum_scatter(returned, "row", scatter_dimension=0, tiled=True)
        depth_grad = lax.psum_scatter(row_grad, "col", scatter_dimension=1, tiled=True)
        depth_grad = depth_grad + from_cols
        cam_total = lax.psum(cam_grad, ("row", "col"))
        depth_now, depth_first, depth_second = adam_step(
            depth_now, depth_grad, depth_first, depth_second, step_number, step_sizes[0]
        )
        camera_now, camera_first, camera_second = adam_step(
            camera_now, cam_total, camera_first, camera_second, step_number, step_sizes[1]
        )
        pair_now, pair_first, pair_second = adam_step(
            pair_now, pair_grad, pair_first, pair_second, step_number, step_sizes[2]
        )
    return (depth_now, camera_now, pair_now)


def pick_lanes(values, index):
    numbers = lax.GatherDimensionNumbers(
        offset_dims=(),
        collapsed_slice_dims=(1,),
        start_index_map=(1,),
        operand_batching_dims=(0,),
        start_indices_batching_dims=(0,),
    )
    return lax.gather(
        values,
        index[..., None],
        numbers,
        slice_sizes=(1, 1),
        mode=lax.GatherScatterMode.PROMISE_IN_BOUNDS,
    )


def cross(a, b):
    return [
        a[1] * b[2] - a[2] * b[1],
        a[2] * b[0] - a[0] * b[2],
        a[0] * b[1] - a[1] * b[0],
    ]


def grad_kernel(shape, step, *refs):
    rows, cols, slots, row_slots, tile = shape
    n_dep = slots + row_slots
    refs = list(refs)
    me, pair, rcam, ccam, rate, x_ref, conf_ref, table, lane_base, ray = refs[:10]
    depth_refs = refs[10 : 10 + n_dep]
    at = 10 + n_dep
    grad_refs = None
    if step > 1:
        grad_refs = refs[at : at + n_dep]
        at += n_dep
    keep_out, send_out = refs[at : at + 2]
    col_out = refs[at + 2 : at + 2 + row_slots]
    at += 2 + row_slots
    pair_out, cam_out = refs[at : at + 2]
    chi_i, chi_j, grad_i, grad_j = refs[at + 2 :]

    i = pl.program_id(0)
    my_row, my_col = me[0], me[1]
    core = my_col & 1
    n_rows = chi_i.shape[1]

    def depth_of(slot, start):
        take = pl.ds(start, tile, stride=SUBLANES)
        value = depth_refs[slot][take, :]
        if step > 1:
            g = grad_refs[slot][take, :]
            value = value - rate[0] * g / (jnp.abs(g) + ADAM_EPS)
        return jnp.exp(value)

    def put_points(dst, cam, base, slot, start, block):
        depth = depth_of(slot, start)
        across = ray[0, block] / cam[base + 12] * depth
        downward = ray[1, block] / cam[base + 12] * depth
        for k in range(3):
            value = (
                cam[base + 3 * k] * across
                + cam[base + 3 * k + 1] * downward
                + cam[base + 3 * k + 2] * depth
                + cam[base + 9 + k]
            )
            dst[k, pl.ds(block * (2 * tile), tile, stride=2), :] = value
            dst[k, pl.ds(block * (2 * tile) + 1, tile, stride=2), :] = value

    def finish(points, grads, side, cam, base, block, sums):
        take = pl.ds(block * (2 * tile) + side, tile, stride=2)
        g = [grads[k, take, :] for k in range(3)]
        v = [points[k, take, :] - cam[base + 9 + k] for k in range(3)]
        axis = [cam[base + 3 * k + 2] for k in range(3)]
        by_depth = g[0] * v[0] + g[1] * v[1] + g[2] * v[2]
        depth = axis[0] * v[0] + axis[1] * v[1] + axis[2] * v[2]
        along = axis[0] * g[0] + axis[1] * g[1] + axis[2] * g[2]
        new = g + cross(v, g) + [by_depth - depth * along]
        return by_depth, [s + n for s, n in zip(sums, new)]

    def stack_sums(sums):
        parts = [jnp.sum(s, axis=0, keepdims=True) for s in sums]
        return jnp.concatenate(parts + [jnp.zeros((1, LANES), jnp.float32)], axis=0)

    def add_camera(image, sums):
        total = jnp.sum(stack_sums(sums), axis=1, keepdims=True)
        lane = lax.broadcasted_iota(jnp.int32, (SUBLANES, LANES), 1)
        cam_out[...] += jnp.where(lane == image, total, 0.0)

    def col_block(e, k_slot):
        return (my_row ^ e) * 2 + (k_slot ^ core)

    @pl.when(i == 0)
    def _():
        def one(j, carry):
            for e in range(row_slots):
                for k_slot in range(2):
                    put_points(
                        chi_j.at[j],
                        ccam,
                        j * 16,
                        slots + e,
                        k_slot * tile * SUBLANES + j,
                        col_block(e, k_slot),
                    )
            return carry

        lax.fori_loop(0, cols, one, 0)
        grad_j[...] = jnp.zeros_like(grad_j)
        cam_out[...] = jnp.zeros_like(cam_out)

    t, m = i // SUBLANES, i % SUBLANES
    for d in range(slots):
        block = my_col ^ d
        t_slot = t ^ core ^ (d & 1)
        put_points(
            chi_i, rcam, i * 16, d, t_slot * tile * SUBLANES + m, block
        )
    grad_i[...] = jnp.zeros_like(grad_i)

    step_rows = 2 * SUBLANES
    is_first = (
        lax.broadcasted_iota(jnp.int32, (step_rows, LANES), 0) % 2
    ) == 0

    def one_pair(j, carry):
        q = i * cols + j
        c = [pair[q * 13 + n] for n in range(13)]
        which = q // TABLE_PAIRS
        lane_at = q % TABLE_PAIRS

        def one_chunk(ch, sums):
            take = pl.ds(pl.multiple_of(ch * step_rows, step_rows), step_rows)
            x = [x_ref[0, j, k, take, :].astype(jnp.float32) for k in range(3)]
            index = lane_base[take, :] + lane_at
            values = table[which, take, :]
            keep = jnp.concatenate(
                [
                    pick_lanes(values[h : h + SUBLANES], index[h : h + SUBLANES])
                    for h in range(0, step_rows, SUBLANES)
                ],
                axis=0,
            )
            weight = conf_ref[0, j, take, :].astype(jnp.float32) * keep
            r = []
            squared = SOFTEN
            for k in range(3):
                turned = c[3 * k] * x[0] + c[3 * k + 1] * x[1] + c[3 * k + 2] * x[2]
                aligned = c[12] * turned + c[9 + k]
                chi = jnp.where(is_first, chi_i[k, take, :], chi_j[j, k, take, :])
                r.append(chi - aligned)
                squared = squared + r[k] * r[k]
            scaled = weight * lax.rsqrt(squared)
            g = [scaled * r[k] for k in range(3)]
            for k in range(3):
                grad_i[k, take, :] += g[k]
                grad_j[j, k, take, :] += g[k]
            new = []
            for k in range(3):
                for l in range(3):
                    new.append(g[k] * x[l])
            new += g
            out = []
            for s, n in zip(sums, new):
                for h in range(0, step_rows, SUBLANES):
                    s = s + n[h : h + SUBLANES]
                out.append(s)
            return tuple(out)

        zero = jnp.zeros((SUBLANES, LANES), jnp.float32)
        sums = lax.fori_loop(0, n_rows // step_rows, one_chunk, (zero,) * 12, unroll=True)
        outer, plain = sums[:9], sums[9:]

        def turned_sum(k, l):
            return (
                outer[3 * k] * c[3 * l]
                + outer[3 * k + 1] * c[3 * l + 1]
                + outer[3 * k + 2] * c[3 * l + 2]
            )

        torque = [
            turned_sum(1, 2) - turned_sum(2, 1),
            turned_sum(2, 0) - turned_sum(0, 2),
            turned_sum(0, 1) - turned_sum(1, 0),
        ]
        trace = turned_sum(0, 0) + turned_sum(1, 1) + turned_sum(2, 2)
        pair_out[0, j] = stack_sums([*plain, *torque, trace])
        return carry

    lax.fori_loop(0, cols, one_pair, 0)

    zero = jnp.zeros((tile, LANES), jnp.float32)
    sums = [zero] * 7
    for d in range(slots):
        block = my_col ^ d
        t_slot = t ^ core ^ (d & 1)
        value, sums = finish(chi_i, grad_i, 0, rcam, i * 16, block, sums)
        out = send_out if d & 1 else keep_out
        start = (d // 2) * (2 * tile * SUBLANES) + t_slot * tile * SUBLANES + m
        out[pl.ds(start, tile, stride=SUBLANES), :] = value
    add_camera(my_row * rows + i, sums)

    @pl.when(i == rows - 1)
    def _():
        def one(j, carry):
            sums = [zero] * 7
            for e in range(row_slots):
                for k_slot in range(2):
                    value, sums = finish(
                        chi_j.at[j], grad_j.at[j], 1, ccam, j * 16, col_block(e, k_slot), sums
                    )
                    start = k_slot * tile * SUBLANES + j
                    col_out[e][pl.ds(start, tile, stride=SUBLANES), :] = value
            add_camera(my_col * cols + j, sums)
            return carry

        lax.fori_loop(0, cols, one, 0)


def grads_of_pairs(step, sizes, me, pair, rcam, ccam, rate, x, conf, table, consts, depths, totals):
    rows, cols, slots, row_slots, tile = sizes
    n_rows = 2 * slots * tile
    smem = pl.BlockSpec(memory_space=pltpu.SMEM)
    vmem = pl.BlockSpec(memory_space=pltpu.VMEM)
    operands = [me, pair, rcam, ccam, rate, x, conf, table, *consts, *depths]
    if step > 1:
        operands += totals
    in_specs = [smem] * 5 + [
        pl.BlockSpec((1, cols, 3, n_rows, LANES), lambda i: (i, 0, 0, 0, 0)),
        pl.BlockSpec((1, cols, n_rows, LANES), lambda i: (i, 0, 0, 0)),
    ]
    in_specs += [vmem] * (len(operands) - len(in_specs))
    block = 2 * tile * SUBLANES
    f32 = jnp.float32
    out_shape = [
        jax.ShapeDtypeStruct((slots // 2 * block, LANES), f32),
        jax.ShapeDtypeStruct((slots // 2 * block, LANES), f32),
        *[jax.ShapeDtypeStruct((block, LANES), f32)] * row_slots,
        jax.ShapeDtypeStruct((rows, cols, SUBLANES, LANES), f32),
        jax.ShapeDtypeStruct((SUBLANES, LANES), f32),
    ]
    out_specs = [vmem] * (2 + row_slots) + [
        pl.BlockSpec((1, cols, SUBLANES, LANES), lambda i: (i, 0, 0, 0)),
        vmem,
    ]
    work = rows * cols * 3 * n_rows * LANES
    return pl.pallas_call(
        functools.partial(grad_kernel, sizes, step),
        grid=(rows,),
        in_specs=in_specs,
        out_specs=out_specs,
        out_shape=out_shape,
        scratch_shapes=[
            pltpu.VMEM((3, n_rows, LANES), f32),
            pltpu.VMEM((cols, 3, n_rows, LANES), f32),
            pltpu.VMEM((3, n_rows, LANES), f32),
            pltpu.VMEM((cols, 3, n_rows, LANES), f32),
        ],
        compiler_params=pltpu.CompilerParams(
            dimension_semantics=("arbitrary",), vmem_limit_bytes=48 * 1024 * 1024
        ),
        cost_estimate=pl.CostEstimate(
            flops=20 * work, bytes_accessed=3 * work, transcendentals=work // 3
        ),
        name=f"pair_grads_{step}",
    )(*operands)


def pair_coefficients(pair_params):
    turned = rotation(pair_params[..., 0:4])
    parts = [turned[k][l] for k in range(3) for l in range(3)]
    parts += [pair_params[..., 4 + k] for k in range(3)]
    parts += [jnp.exp(pair_params[..., 7])]
    return jnp.stack(parts, axis=-1)


def quaternion_grad(quaternion, torque):
    length = jnp.sqrt(jnp.sum(quaternion * quaternion, axis=-1, keepdims=True))
    factor = 2.0 / (length * length)
    w, v = quaternion[..., 0:1], [quaternion[..., k : k + 1] for k in (1, 2, 3)]
    t = [torque[..., k : k + 1] for k in range(3)]
    c = cross(t, v)
    real = -(t[0] * v[0] + t[1] * v[1] + t[2] * v[2])
    return [factor * real] + [factor * (w * t[k] + c[k]) for k in range(3)]


def pair_grads(pair_params, sums):
    scale = jnp.exp(pair_params[..., 7:8])
    parts = quaternion_grad(pair_params[..., 0:4], scale * sums[..., 3:6])
    parts += [-sums[..., 0:3], -scale * sums[..., 6:7]]
    return jnp.concatenate(parts, axis=-1)


def camera_grads(cameras, sums):
    parts = quaternion_grad(cameras[:, 0:4], sums[:, 3:6])
    return jnp.concatenate(parts + [sums[:, 0:3], -sums[:, 6:7]], axis=-1)


def camera_rotation(cameras):
    turned = rotation(cameras[:, 0:4])
    return jnp.stack([turned[k][l] for k in range(3) for l in range(3)], axis=-1)


def camera_coefficients(cameras):
    turned = camera_rotation(cameras)
    focal = jnp.exp(cameras[:, 7:8])
    pad = jnp.zeros((cameras.shape[0], 3), jnp.float32)
    return jnp.concatenate([turned, cameras[:, 4:7], focal, pad], axis=1)


def pixel_constants(n_tiles, blocks):
    pixel = np.arange(n_tiles * LANES).reshape(n_tiles, LANES)
    line = pixel // IMG_WIDTH
    across = (pixel % IMG_WIDTH).astype(np.float32) - np.float32((IMG_WIDTH - 1) / 2.0)
    downward = (line + (IMG_HEIGHT - WIN_ROWS) // 2).astype(np.float32) - np.float32(
        (IMG_HEIGHT - 1) / 2.0
    )
    ray = np.stack([across, downward]).reshape(2, blocks, n_tiles // blocks, LANES)
    first = line[:, 0]
    base = (line != first[:, None]).astype(np.int32) * TABLE_PAIRS
    base = np.repeat(base, 2, axis=0)
    lines = np.stack([first, np.minimum(first + 1, WIN_ROWS - 1)])
    pick = (lines[:, :, None] == np.arange(WIN_ROWS)).astype(np.float32)
    return jnp.asarray(base), jnp.asarray(ray), np.repeat(pick, 2, axis=1)


def tree_sum(parts):
    while len(parts) > 1:
        parts = [a + b for a, b in zip(parts[::2], parts[1::2])]
    return parts[0]


def xor_permute(value, axis, bit, size):
    return lax.ppermute(value, axis, [(c, c ^ bit) for c in range(size)])


def fast_body(n_row, n_col, pointmaps, confidence, valid_blocks, log_depth, camera, pair_pose, step_sizes):
    rows, cols = pointmaps.shape[:2]
    pixels = pointmaps.shape[4]
    n_tiles = pixels // LANES
    tile = n_tiles // n_col
    sizes = (rows, cols, n_col, n_row, tile)
    row_index = lax.axis_index("row")
    col_index = lax.axis_index("col")
    core = col_index % 2
    me = jnp.stack([row_index, col_index]).astype(jnp.int32)
    f32 = jnp.float32

    x = pointmaps.transpose(0, 1, 3, 2, 4).reshape(rows, cols, 3, 2, n_tiles, LANES)
    x = x.transpose(0, 1, 2, 4, 3, 5).reshape(rows, cols, 3, 2 * n_tiles, LANES)
    conf = confidence.reshape(rows, cols, 2, n_tiles, LANES)
    conf = conf.transpose(0, 1, 3, 2, 4).reshape(rows, cols, 2 * n_tiles, LANES)

    base, ray, pick = pixel_constants(n_tiles, n_col)
    first_ids = row_index * rows + jnp.arange(rows, dtype=jnp.int32)
    second_ids = col_index * cols + jnp.arange(cols, dtype=jnp.int32)
    different = (first_ids[:, None] != second_ids[None, :]).astype(f32)
    share = different / (2.0 * (IMAGES - 1))
    valid = (valid_blocks.astype(f32)).reshape(rows * cols, WIN_ROWS)
    picked = lax.dot_general(
        jnp.asarray(pick.reshape(-1, WIN_ROWS)), valid, (((1,), (1,)), ((), ()))
    )
    picked = picked * share.reshape(1, rows * cols)
    picked = picked.reshape(2, 2 * n_tiles, rows * cols // TABLE_PAIRS, TABLE_PAIRS)
    table = picked.transpose(2, 1, 0, 3).reshape(-1, 2 * n_tiles, 2 * TABLE_PAIRS)

    def relative(value):
        return jnp.where(core == 0, value, value[::-1])

    def swap_perm(m):
        pairs = []
        for r in range(n_row):
            for c in range(n_col):
                to = (c // 2) * n_col + 2 * r + (m ^ (c & 1))
                pairs.append((r * n_col + c, to))
        return pairs

    def exchange(value, m):
        return lax.ppermute(value, ("row", "col"), swap_perm(m))

    def spread(row_part, col_part):
        own, other, down = [row_part], [], [col_part]
        for d in range(1, n_col // 2):
            own.append(xor_permute(row_part, "col", 2 * d, n_col))
        for e in range(1, n_row):
            down.append(xor_permute(col_part, "row", e, n_row))
        for d in range(n_col // 2):
            other.append(xor_permute(own[d], "col", 1, n_col))
        flat = []
        for d in range(n_col // 2):
            flat += [own[d], other[d]]
        return flat + down

    block = 2 * tile * SUBLANES

    def reduce_blocks(keep, send, cam, col_parts):
        got = xor_permute(send, "col", 1, n_col)
        cam = cam + xor_permute(cam, "col", 1, n_col)
        total = (keep + got).reshape(n_col // 2, block, LANES)
        col_total = col_parts[0]
        for e in range(1, n_row):
            col_total = col_total + xor_permute(col_parts[e], "row", e, n_row)
        row_total, cams = total[0], [cam]
        for d in range(1, n_col // 2):
            message = jnp.concatenate([total[d], cam], axis=0)
            message = xor_permute(message, "col", 2 * d, n_col)
            row_total = row_total + message[:block]
            cams.append(message[block:])
        cam_total = tree_sum(cams)
        row_total = row_total.reshape(2, tile, SUBLANES, LANES)
        col_total = col_total.reshape(2, tile, SUBLANES, LANES)
        return row_total, col_total, cam_total

    depth = log_depth.reshape(2, SUBLANES, tile, LANES).transpose(0, 2, 1, 3)
    depth = relative(depth)
    col_depth = jnp.stack([exchange(depth[m], m) for m in range(2)])
    depths = spread(depth.reshape(-1, LANES), col_depth.reshape(-1, LANES))

    camera_now, pair_now = camera, pair_pose
    camera_state = (jnp.zeros_like(camera),) * 2
    pair_state = (jnp.zeros_like(pair_pose),) * 2
    totals = None
    block_totals = []
    for step in range(1, ADAM_STEPS + 1):
        coeffs = camera_coefficients(camera_now)
        rcam = lax.dynamic_slice_in_dim(coeffs, row_index * rows, rows, 0)
        ccam = lax.dynamic_slice_in_dim(coeffs, col_index * cols, cols, 0)
        coef = pair_coefficients(pair_now)
        outs = grads_of_pairs(
            step,
            sizes,
            me,
            coef.reshape(-1),
            rcam.reshape(-1),
            ccam.reshape(-1),
            step_sizes,
            x,
            conf,
            table,
            (base, ray),
            depths,
            totals,
        )
        keep, send = outs[:2]
        col_parts = outs[2 : 2 + n_row]
        pair_sums, cam_sums = outs[2 + n_row :]
        row_total, col_total, cam_sums = reduce_blocks(keep, send, cam_sums, col_parts)
        if step < ADAM_STEPS:
            received = [
                exchange(jnp.stack([row_total[m], col_total[m]]), m) for m in range(2)
            ]
            total = row_total + jnp.stack([v[1] for v in received])
            col_total = col_total + jnp.stack([v[0] for v in received])
            message = jnp.concatenate([col_total.reshape(-1, LANES), cam_sums], axis=0)
            totals = spread(total.reshape(-1, LANES), message)
            cam_sums = tree_sum([v[block:] for v in totals[n_col:]])
        else:
            received = [exchange(col_total[m], m) for m in range(2)]
            total = row_total + jnp.stack(received)
            others = [xor_permute(cam_sums, "row", e, n_row) for e in range(1, n_row)]
            cam_sums = tree_sum([cam_sums, *others])
        block_totals.append(total)
        cam_grad = camera_grads(camera_now, cam_sums.T[:IMAGES])
        camera_now, *camera_state = adam_step(
            camera_now, cam_grad, *camera_state, step, step_sizes[1]
        )
        pair_grad = pair_grads(pair_now, jnp.sum(pair_sums, axis=-1))
        pair_now, *pair_state = adam_step(pair_now, pair_grad, *pair_state, step, step_sizes[2])

    depth_now = depth
    depth_state = (jnp.zeros_like(depth),) * 2
    for step in range(1, ADAM_STEPS + 1):
        depth_now, *depth_state = adam_step(
            depth_now, block_totals[step - 1], *depth_state, step, step_sizes[0]
        )
    depth_now = relative(depth_now).transpose(0, 2, 1, 3).reshape(log_depth.shape)
    return depth_now, camera_now, pair_now


def solution(mesh):
    n_row, n_col = mesh.shape["row"], mesh.shape["col"]
    in_specs = (
        P("row", "col", None, None, None),
        P("row", "col", None, None),
        P("row", "col", None),
        P("row", "col"),
        P(),
        P("row", "col", None),
        P(),
    )
    out_specs = (P("row", "col"), P(), P("row", "col", None))

    def body(pointmaps, *rest):
        rows, cols, pixels = pointmaps.shape[0], pointmaps.shape[1], pointmaps.shape[4]
        whole_tiles = pixels % (LANES * n_col) == 0 and (2 * pixels // LANES) % 16 == 0
        whole_tables = (rows * cols) % TABLE_PAIRS == 0
        paired = IMAGES <= LANES and rows == 2 * SUBLANES and cols == SUBLANES and n_col == 2 * n_row
        power = n_row & (n_row - 1) == 0
        if whole_tiles and whole_tables and paired and power:
            return fast_body(n_row, n_col, pointmaps, *rest)
        return general_body(pointmaps, *rest)

    return jax.shard_map(body, mesh=mesh, in_specs=in_specs, out_specs=out_specs, check_vma=False)
```

```python
import functools

import numpy as np

import jax
import jax.numpy as jnp
from jax import lax
from jax.experimental import pallas as pl
from jax.experimental.pallas import tpu as pltpu
from jax.sharding import PartitionSpec as P

IMAGES = 64
IMG_WIDTH = 224
IMG_HEIGHT = 224
WIN_ROWS = 64
ADAM_STEPS = 2

BETA_ONE = 0.9
BETA_TWO = 0.999
ADAM_EPS = 0.001
SOFTEN = 0.01

LANES = 128
SUBLANES = 8
TABLE_PAIRS = 64


def rotation(quaternion):
    length = jnp.sqrt(jnp.sum(quaternion * quaternion, axis=-1))
    w = quaternion[..., 0] / length
    x = quaternion[..., 1] / length
    y = quaternion[..., 2] / length
    z = quaternion[..., 3] / length
    return [
        [1.0 - 2.0 * (y * y + z * z), 2.0 * (x * y - w * z), 2.0 * (x * z + w * y)],
        [2.0 * (x * y + w * z), 1.0 - 2.0 * (x * x + z * z), 2.0 * (y * z - w * x)],
        [2.0 * (x * z - w * y), 2.0 * (y * z + w * x), 1.0 - 2.0 * (x * x + y * y)],
    ]


def adam_step(param, grad, first, second, step_number, step_size):
    first = BETA_ONE * first + (1.0 - BETA_ONE) * grad
    second = BETA_TWO * second + (1.0 - BETA_TWO) * grad * grad
    update = (
        step_size
        * (first / (1.0 - BETA_ONE**step_number))
        / (jnp.sqrt(second / (1.0 - BETA_TWO**step_number)) + ADAM_EPS)
    )
    return (param - update, first, second)


def world_points(log_depths, cameras):
    pixel_count = log_depths.shape[-1]
    position = jnp.arange(pixel_count, dtype=jnp.int32)
    across = (position % IMG_WIDTH).astype(jnp.float32) - (IMG_WIDTH - 1) / 2.0
    downward = (position // IMG_WIDTH + (IMG_HEIGHT - WIN_ROWS) // 2).astype(jnp.float32) - (
        IMG_HEIGHT - 1
    ) / 2.0
    focal_len = jnp.exp(cameras[:, 7:8])
    depth_map = jnp.exp(log_depths)
    ray_parts = (
        across[None, :] / focal_len * depth_map,
        downward[None, :] / focal_len * depth_map,
        depth_map,
    )
    turned = rotation(cameras[:, 0:4])
    return [
        turned[k][0][:, None] * ray_parts[0]
        + turned[k][1][:, None] * ray_parts[1]
        + turned[k][2][:, None] * ray_parts[2]
        + cameras[:, 4 + k][:, None]
        for k in range(3)
    ]


def pair_loss(
    first_depth,
    second_depth,
    first_camera,
    second_camera,
    pair_params,
    pointmaps,
    confidence,
    valid_blocks,
    first_ids,
    second_ids,
):
    first_world = world_points(first_depth, first_camera)
    second_world = world_points(second_depth, second_camera)
    pair_rotation = rotation(pair_params[..., 0:4])
    pair_scale = jnp.exp(pair_params[..., 7])
    pair_keep = (first_ids[:, None] != second_ids[None, :]).astype(jnp.float32)
    pixel_keep = (
        jnp.repeat(valid_blocks.astype(jnp.float32), IMG_WIDTH, axis=2) * pair_keep[:, :, None]
    )
    loss_sum = jnp.zeros((), jnp.float32)
    for side_index in range(2):
        if side_index == 0:
            points_side = [first_world[k][:, None, :] for k in range(3)]
        else:
            points_side = [second_world[k][None, :, :] for k in range(3)]
        source = [pointmaps[:, :, side_index, k, :].astype(jnp.float32) for k in range(3)]
        squared = SOFTEN
        for k in range(3):
            aligned = (
                pair_scale[..., None]
                * (
                    pair_rotation[k][0][..., None] * source[0]
                    + pair_rotation[k][1][..., None] * source[1]
                    + pair_rotation[k][2][..., None] * source[2]
                )
                + pair_params[..., 4 + k][..., None]
            )
            residual = points_side[k] - aligned
            squared = squared + residual * residual
        weight = confidence[:, :, side_index, :].astype(jnp.float32) * pixel_keep
        loss_sum = loss_sum + jnp.sum(weight * jnp.sqrt(squared))
    return loss_sum / (2.0 * (IMAGES - 1))


def general_body(pointmaps, confidence, valid_blocks, log_depth, camera, pair_pose, step_sizes):
    row_count = pointmaps.shape[0]
    col_count = pointmaps.shape[1]
    row_index = lax.axis_index("row")
    col_index = lax.axis_index("col")
    first_ids = row_index * row_count + jnp.arange(row_count, dtype=jnp.int32)
    second_ids = col_index * col_count + jnp.arange(col_count, dtype=jnp.int32)

    def local_loss(row_depth, col_depth, cameras, pair_params):
        first_camera = lax.dynamic_slice_in_dim(cameras, row_index * row_count, row_count, 0)
        second_camera = lax.dynamic_slice_in_dim(cameras, col_index * col_count, col_count, 0)
        return pair_loss(
            row_depth,
            col_depth,
            first_camera,
            second_camera,
            pair_params,
            pointmaps,
            confidence,
            valid_blocks,
            first_ids,
            second_ids,
        )

    depth_now, camera_now, pair_now = (log_depth, camera, pair_pose)
    depth_first = jnp.zeros_like(log_depth)
    depth_second = jnp.zeros_like(log_depth)
    camera_first = jnp.zeros_like(camera)
    camera_second = jnp.zeros_like(camera)
    pair_first = jnp.zeros_like(pair_pose)
    pair_second = jnp.zeros_like(pair_pose)
    for step_number in range(1, ADAM_STEPS + 1):
        row_depth = lax.all_gather(depth_now, "col", axis=1, tiled=True)
        every_image = lax.all_gather(depth_now, "row", axis=0, tiled=True)
        col_depth = lax.all_to_all(every_image, "col", split_axis=0, concat_axis=1, tiled=True)
        row_grad, col_grad, cam_grad, pair_grad = jax.grad(local_loss, argnums=(0, 1, 2, 3))(
            row_depth, col_depth, camera_now, pair_now
        )
        returned = lax.all_to_all(col_grad, "col", split_axis=1, concat_axis=0, tiled=True)
        from_cols = lax.psum_scatter(returned, "row", scatter_dimension=0, tiled=True)
        depth_grad = lax.psum_scatter(row_grad, "col", scatter_dimension=1, tiled=True)
        depth_grad = depth_grad + from_cols
        cam_total = lax.psum(cam_grad, ("row", "col"))
        depth_now, depth_first, depth_second = adam_step(
            depth_now, depth_grad, depth_first, depth_second, step_number, step_sizes[0]
        )
        camera_now, camera_first, camera_second = adam_step(
            camera_now, cam_total, camera_first, camera_second, step_number, step_sizes[1]
        )
        pair_now, pair_first, pair_second = adam_step(
            pair_now, pair_grad, pair_first, pair_second, step_number, step_sizes[2]
        )
    return (depth_now, camera_now, pair_now)


def pick_lanes(values, index):
    numbers = lax.GatherDimensionNumbers(
        offset_dims=(),
        collapsed_slice_dims=(1,),
        start_index_map=(1,),
        operand_batching_dims=(0,),
        start_indices_batching_dims=(0,),
    )
    return lax.gather(
        values,
        index[..., None],
        numbers,
        slice_sizes=(1, 1),
        mode=lax.GatherScatterMode.PROMISE_IN_BOUNDS,
    )


def cross(a, b):
    return [
        a[1] * b[2] - a[2] * b[1],
        a[2] * b[0] - a[0] * b[2],
        a[0] * b[1] - a[1] * b[0],
    ]


def grad_kernel(shape, step, *refs):
    rows, cols, slots, row_slots, tile = shape
    n_dep = slots + row_slots
    refs = list(refs)
    me, pair, cam, rate, x_ref, conf_ref, table, lane_base, ray = refs[:9]
    depth_refs = refs[9 : 9 + n_dep]
    at = 9 + n_dep
    grad_refs = None
    if step > 1:
        grad_refs = refs[at : at + n_dep]
        at += n_dep
    keep_out, send_out = refs[at : at + 2]
    col_out = refs[at + 2 : at + 2 + row_slots]
    at += 2 + row_slots
    pair_out, cam_out = refs[at : at + 2]
    chi_i, chi_j, grad_i, grad_j = refs[at + 2 :]

    i = pl.program_id(0)
    my_row, my_col = me[0], me[1]
    core = my_col & 1
    n_rows = chi_i.shape[1]

    def depth_of(slot, start):
        take = pl.ds(start, tile, stride=SUBLANES)
        value = depth_refs[slot][take, :]
        if step > 1:
            g = grad_refs[slot][take, :]
            value = value - rate[0] * g / (jnp.abs(g) + ADAM_EPS)
        return jnp.exp(value)

    def put_points(dst, image, slot, start, block):
        depth = depth_of(slot, start)
        across = ray[0, block] / cam[12, image] * depth
        downward = ray[1, block] / cam[12, image] * depth
        for k in range(3):
            value = (
                cam[3 * k, image] * across
                + cam[3 * k + 1, image] * downward
                + cam[3 * k + 2, image] * depth
                + cam[9 + k, image]
            )
            dst[k, pl.ds(block * (2 * tile), tile, stride=2), :] = value
            dst[k, pl.ds(block * (2 * tile) + 1, tile, stride=2), :] = value

    def finish(points, grads, side, image, block, sums):
        take = pl.ds(block * (2 * tile) + side, tile, stride=2)
        g = [grads[k, take, :] for k in range(3)]
        v = [points[k, take, :] - cam[9 + k, image] for k in range(3)]
        axis = [cam[3 * k + 2, image] for k in range(3)]
        by_depth = g[0] * v[0] + g[1] * v[1] + g[2] * v[2]
        depth = axis[0] * v[0] + axis[1] * v[1] + axis[2] * v[2]
        along = axis[0] * g[0] + axis[1] * g[1] + axis[2] * g[2]
        new = g + cross(v, g) + [by_depth - depth * along]
        return by_depth, [s + n for s, n in zip(sums, new)]

    def stack_sums(sums):
        parts = [jnp.sum(s, axis=0, keepdims=True) for s in sums]
        return jnp.concatenate(parts + [jnp.zeros((1, LANES), jnp.float32)], axis=0)

    def add_camera(image, sums):
        total = jnp.sum(stack_sums(sums), axis=1, keepdims=True)
        lane = lax.broadcasted_iota(jnp.int32, (SUBLANES, LANES), 1)
        cam_out[...] += jnp.where(lane == image, total, 0.0)

    def col_block(e, k_slot):
        return (my_row ^ e) * 2 + (k_slot ^ core)

    @pl.when(i == 0)
    def _():
        def one(j, carry):
            for e in range(row_slots):
                for k_slot in range(2):
                    put_points(
                        chi_j.at[j],
                        my_col * cols + j,
                        slots + e,
                        k_slot * tile * SUBLANES + j,
                        col_block(e, k_slot),
                    )
            return carry

        lax.fori_loop(0, cols, one, 0)
        grad_j[...] = jnp.zeros_like(grad_j)
        cam_out[...] = jnp.zeros_like(cam_out)

    t, m = i // SUBLANES, i % SUBLANES
    for d in range(slots):
        block = my_col ^ d
        t_slot = t ^ core ^ (d & 1)
        put_points(
            chi_i, my_row * rows + i, d, t_slot * tile * SUBLANES + m, block
        )
    grad_i[...] = jnp.zeros_like(grad_i)

    step_rows = 2 * SUBLANES
    is_first = (
        lax.broadcasted_iota(jnp.int32, (step_rows, LANES), 0) % 2
    ) == 0

    def one_pair(j, carry):
        q = i * cols + j
        c = [pair[j, n, i] for n in range(13)]
        which = q // TABLE_PAIRS
        lane_at = q % TABLE_PAIRS

        def one_chunk(ch, sums):
            take = pl.ds(pl.multiple_of(ch * step_rows, step_rows), step_rows)
            x = [x_ref[0, j, k, take, :].astype(jnp.float32) for k in range(3)]
            index = lane_base[take, :] + lane_at
            values = table[which, take, :]
            keep = jnp.concatenate(
                [
                    pick_lanes(values[h : h + SUBLANES], index[h : h + SUBLANES])
                    for h in range(0, step_rows, SUBLANES)
                ],
                axis=0,
            )
            weight = conf_ref[0, j, take, :].astype(jnp.float32) * keep
            r = []
            squared = SOFTEN
            for k in range(3):
                turned = c[3 * k] * x[0] + c[3 * k + 1] * x[1] + c[3 * k + 2] * x[2]
                aligned = c[12] * turned + c[9 + k]
                chi = jnp.where(is_first, chi_i[k, take, :], chi_j[j, k, take, :])
                r.append(chi - aligned)
                squared = squared + r[k] * r[k]
            scaled = weight * lax.rsqrt(squared)
            g = [scaled * r[k] for k in range(3)]
            for k in range(3):
                grad_i[k, take, :] += g[k]
                grad_j[j, k, take, :] += g[k]
            new = []
            for k in range(3):
                for l in range(3):
                    new.append(g[k] * x[l])
            new += g
            out = []
            for s, n in zip(sums, new):
                for h in range(0, step_rows, SUBLANES):
                    s = s + n[h : h + SUBLANES]
                out.append(s)
            return tuple(out)

        zero = jnp.zeros((SUBLANES, LANES), jnp.float32)
        sums = lax.fori_loop(0, n_rows // step_rows, one_chunk, (zero,) * 12, unroll=True)
        outer, plain = sums[:9], sums[9:]

        def turned_sum(k, l):
            return (
                outer[3 * k] * c[3 * l]
                + outer[3 * k + 1] * c[3 * l + 1]
                + outer[3 * k + 2] * c[3 * l + 2]
            )

        torque = [
            turned_sum(1, 2) - turned_sum(2, 1),
            turned_sum(2, 0) - turned_sum(0, 2),
            turned_sum(0, 1) - turned_sum(1, 0),
        ]
        trace = turned_sum(0, 0) + turned_sum(1, 1) + turned_sum(2, 2)
        pair_out[0, j] = stack_sums([*plain, *torque, trace])
        return carry

    lax.fori_loop(0, cols, one_pair, 0)

    zero = jnp.zeros((tile, LANES), jnp.float32)
    sums = [zero] * 7
    for d in range(slots):
        block = my_col ^ d
        t_slot = t ^ core ^ (d & 1)
        value, sums = finish(chi_i, grad_i, 0, my_row * rows + i, block, sums)
        out = send_out if d & 1 else keep_out
        start = (d // 2) * (2 * tile * SUBLANES) + t_slot * tile * SUBLANES + m
        out[pl.ds(start, tile, stride=SUBLANES), :] = value
    add_camera(my_row * rows + i, sums)

    @pl.when(i == rows - 1)
    def _():
        def one(j, carry):
            sums = [zero] * 7
            for e in range(row_slots):
                for k_slot in range(2):
                    value, sums = finish(
                        chi_j.at[j], grad_j.at[j], 1, my_col * cols + j, col_block(e, k_slot), sums
                    )
                    start = k_slot * tile * SUBLANES + j
                    col_out[e][pl.ds(start, tile, stride=SUBLANES), :] = value
            add_camera(my_col * cols + j, sums)
            return carry

        lax.fori_loop(0, cols, one, 0)


def grads_of_pairs(step, sizes, me, pair, cam, rate, x, conf, table, consts, depths, totals):
    rows, cols, slots, row_slots, tile = sizes
    n_rows = 2 * slots * tile
    smem = pl.BlockSpec(memory_space=pltpu.SMEM)
    vmem = pl.BlockSpec(memory_space=pltpu.VMEM)
    operands = [me, pair, cam, rate, x, conf, table, *consts, *depths]
    if step > 1:
        operands += totals
    in_specs = [smem] * 4 + [
        pl.BlockSpec((1, cols, 3, n_rows, LANES), lambda i: (i, 0, 0, 0, 0)),
        pl.BlockSpec((1, cols, n_rows, LANES), lambda i: (i, 0, 0, 0)),
    ]
    in_specs += [vmem] * (len(operands) - len(in_specs))
    block = 2 * tile * SUBLANES
    f32 = jnp.float32
    out_shape = [
        jax.ShapeDtypeStruct((slots // 2 * block, LANES), f32),
        jax.ShapeDtypeStruct((slots // 2 * block, LANES), f32),
        *[jax.ShapeDtypeStruct((block, LANES), f32)] * row_slots,
        jax.ShapeDtypeStruct((rows, cols, SUBLANES, LANES), f32),
        jax.ShapeDtypeStruct((SUBLANES, LANES), f32),
    ]
    out_specs = [vmem] * (2 + row_slots) + [
        pl.BlockSpec((1, cols, SUBLANES, LANES), lambda i: (i, 0, 0, 0)),
        vmem,
    ]
    work = rows * cols * 3 * n_rows * LANES
    return pl.pallas_call(
        functools.partial(grad_kernel, sizes, step),
        grid=(rows,),
        in_specs=in_specs,
        out_specs=out_specs,
        out_shape=out_shape,
        scratch_shapes=[
            pltpu.VMEM((3, n_rows, LANES), f32),
            pltpu.VMEM((cols, 3, n_rows, LANES), f32),
            pltpu.VMEM((3, n_rows, LANES), f32),
            pltpu.VMEM((cols, 3, n_rows, LANES), f32),
        ],
        compiler_params=pltpu.CompilerParams(
            dimension_semantics=("arbitrary",), vmem_limit_bytes=52 * 1024 * 1024
        ),
        cost_estimate=pl.CostEstimate(
            flops=20 * work, bytes_accessed=3 * work, transcendentals=work // 3
        ),
        name=f"pair_grads_{step}",
    )(*operands)


def rotation_of(q):
    length = jnp.sqrt(q[0] * q[0] + q[1] * q[1] + q[2] * q[2] + q[3] * q[3])
    w, x, y, z = (part / length for part in q)
    return [
        1.0 - 2.0 * (y * y + z * z),
        2.0 * (x * y - w * z),
        2.0 * (x * z + w * y),
        2.0 * (x * y + w * z),
        1.0 - 2.0 * (x * x + z * z),
        2.0 * (y * z - w * x),
        2.0 * (x * z - w * y),
        2.0 * (y * z + w * x),
        1.0 - 2.0 * (x * x + y * y),
    ]


def quaternion_grad(q, torque):
    w, v = q[0], q[1:4]
    factor = 2.0 / (w * w + v[0] * v[0] + v[1] * v[1] + v[2] * v[2])
    c = cross(torque, v)
    real = -(torque[0] * v[0] + torque[1] * v[1] + torque[2] * v[2])
    return [factor * real] + [factor * (w * torque[k] + c[k]) for k in range(3)]


def pair_grads(p, s):
    scale = jnp.exp(p[7])
    parts = quaternion_grad(p, [scale * s[k] for k in (3, 4, 5)])
    return parts + [-s[0], -s[1], -s[2], -scale * s[6]]


def camera_grads(p, s):
    return quaternion_grad(p, s[3:6]) + [s[0], s[1], s[2], -s[6]]


def update_kernel(grads_of, step, n_sums, axes, *refs):
    refs = list(refs)
    rate, params = refs[:2]

    def at(ref, k):
        return ref.at[:, k, :] if axes == 3 else ref.at[pl.ds(k, 1), :]

    p = [at(params, k)[...] for k in range(8)]
    rest = refs[2:]
    if step:
        width = p[0].shape[-1]
        parts = []
        for sums in rest[:n_sums]:
            top = sums.shape[-2] - SUBLANES
            if axes == 3:
                parts.append([sums[:, k, :] for k in range(7)])
            else:
                parts.append([sums[pl.ds(top + k, 1), pl.ds(0, width)] for k in range(7)])
        total = [tree_sum([part[k] for part in parts]) for k in range(7)]
        g = grads_of(p, total)
        rest = rest[n_sums:]
        first, second = [jnp.zeros_like(v) for v in p], [jnp.zeros_like(v) for v in p]
        if step > 1:
            first = [at(rest[0], k)[...] for k in range(8)]
            second = [at(rest[1], k)[...] for k in range(8)]
            rest = rest[2:]
        for k in range(8):
            p[k], first[k], second[k] = adam_step(p[k], g[k], first[k], second[k], step, rate[0])
            at(rest[0], k)[...] = p[k]
            if step < ADAM_STEPS:
                at(rest[1], k)[...] = first[k]
                at(rest[2], k)[...] = second[k]
        rest = rest[3:] if step < ADAM_STEPS else rest[1:]
    if step < ADAM_STEPS:
        values = rotation_of(p[0:4]) + p[4:7] + [jnp.exp(p[7])]
        for k, value in enumerate(values):
            at(rest[0], k)[...] = value


def update(grads_of, step, rate, params, sums, state, name):
    f32 = jnp.float32
    like = jax.ShapeDtypeStruct(params.shape, f32)
    coef_shape = (*params.shape[:-2], 16, params.shape[-1])
    out_shape = []
    if step:
        out_shape += [like] * (3 if step < ADAM_STEPS else 1)
    if step < ADAM_STEPS:
        out_shape.append(jax.ShapeDtypeStruct(coef_shape, f32))
    vmem = pl.BlockSpec(memory_space=pltpu.VMEM)
    operands = [params, *sums, *(state if step > 1 else [])]
    outs = pl.pallas_call(
        functools.partial(update_kernel, grads_of, step, len(sums), params.ndim),
        in_specs=[pl.BlockSpec(memory_space=pltpu.SMEM)] + [vmem] * len(operands),
        out_specs=[vmem] * len(out_shape),
        out_shape=out_shape,
        compiler_params=pltpu.CompilerParams(vmem_limit_bytes=4 * 1024 * 1024),
        cost_estimate=pl.CostEstimate(flops=10000, bytes_accessed=100000, transcendentals=0),
        name=f"{name}_{step}",
    )(rate, *operands)
    if not step:
        return params, [], outs[0]
    if step < ADAM_STEPS:
        return outs[0], outs[1:3], outs[3]
    return outs[0], [], None


def pixel_constants(n_tiles, blocks):
    pixel = np.arange(n_tiles * LANES).reshape(n_tiles, LANES)
    line = pixel // IMG_WIDTH
    across = (pixel % IMG_WIDTH).astype(np.float32) - np.float32((IMG_WIDTH - 1) / 2.0)
    downward = (line + (IMG_HEIGHT - WIN_ROWS) // 2).astype(np.float32) - np.float32(
        (IMG_HEIGHT - 1) / 2.0
    )
    ray = np.stack([across, downward]).reshape(2, blocks, n_tiles // blocks, LANES)
    first = line[:, 0]
    base = (line != first[:, None]).astype(np.int32) * TABLE_PAIRS
    base = np.repeat(base, 2, axis=0)
    lines = np.stack([first, np.minimum(first + 1, WIN_ROWS - 1)])
    pick = (lines[:, :, None] == np.arange(WIN_ROWS)).astype(np.float32)
    return jnp.asarray(base), jnp.asarray(ray), np.repeat(pick, 2, axis=1)


def tree_sum(parts):
    while len(parts) > 1:
        parts = [a + b for a, b in zip(parts[::2], parts[1::2])]
    return parts[0]


def xor_permute(value, axis, bit, size):
    return lax.ppermute(value, axis, [(c, c ^ bit) for c in range(size)])


def fast_body(n_row, n_col, pointmaps, confidence, valid_blocks, log_depth, camera, pair_pose, step_sizes):
    rows, cols = pointmaps.shape[:2]
    pixels = pointmaps.shape[4]
    n_tiles = pixels // LANES
    tile = n_tiles // n_col
    sizes = (rows, cols, n_col, n_row, tile)
    row_index = lax.axis_index("row")
    col_index = lax.axis_index("col")
    core = col_index % 2
    me = jnp.stack([row_index, col_index]).astype(jnp.int32)
    f32 = jnp.float32

    x = pointmaps.transpose(0, 1, 3, 2, 4).reshape(rows, cols, 3, 2, n_tiles, LANES)
    x = x.transpose(0, 1, 2, 4, 3, 5).reshape(rows, cols, 3, 2 * n_tiles, LANES)
    conf = confidence.reshape(rows, cols, 2, n_tiles, LANES)
    conf = conf.transpose(0, 1, 3, 2, 4).reshape(rows, cols, 2 * n_tiles, LANES)

    base, ray, pick = pixel_constants(n_tiles, n_col)
    first_ids = row_index * rows + jnp.arange(rows, dtype=jnp.int32)
    second_ids = col_index * cols + jnp.arange(cols, dtype=jnp.int32)
    different = (first_ids[:, None] != second_ids[None, :]).astype(f32)
    share = different / (2.0 * (IMAGES - 1))
    valid = (valid_blocks.astype(f32)).reshape(rows * cols, WIN_ROWS)
    picked = lax.dot_general(
        jnp.asarray(pick.reshape(-1, WIN_ROWS)), valid, (((1,), (1,)), ((), ()))
    )
    picked = picked * share.reshape(1, rows * cols)
    picked = picked.reshape(2, 2 * n_tiles, rows * cols // TABLE_PAIRS, TABLE_PAIRS)
    table = picked.transpose(2, 1, 0, 3).reshape(-1, 2 * n_tiles, 2 * TABLE_PAIRS)

    def relative(value):
        return jnp.where(core == 0, value, value[::-1])

    def swap_perm(m):
        pairs = []
        for r in range(n_row):
            for c in range(n_col):
                to = (c // 2) * n_col + 2 * r + (m ^ (c & 1))
                pairs.append((r * n_col + c, to))
        return pairs

    def exchange(value, m):
        return lax.ppermute(value, ("row", "col"), swap_perm(m))

    def spread(row_part, col_part):
        own, other, down = [row_part], [], [col_part]
        for d in range(1, n_col // 2):
            own.append(xor_permute(row_part, "col", 2 * d, n_col))
        for e in range(1, n_row):
            down.append(xor_permute(col_part, "row", e, n_row))
        for d in range(n_col // 2):
            other.append(xor_permute(own[d], "col", 1, n_col))
        flat = []
        for d in range(n_col // 2):
            flat += [own[d], other[d]]
        return flat + down

    block = 2 * tile * SUBLANES

    def reduce_blocks(keep, send, cam, col_parts):
        got = xor_permute(send, "col", 1, n_col)
        cam = cam + xor_permute(cam, "col", 1, n_col)
        total = (keep + got).reshape(n_col // 2, block, LANES)
        col_total = col_parts[0]
        for e in range(1, n_row):
            col_total = col_total + xor_permute(col_parts[e], "row", e, n_row)
        row_total, cams = total[0], [cam]
        for d in range(1, n_col // 2):
            message = jnp.concatenate([total[d], cam], axis=0)
            message = xor_permute(message, "col", 2 * d, n_col)
            row_total = row_total + message[:block]
            cams.append(message[block:])
        cam_total = tree_sum(cams)
        row_total = row_total.reshape(2, tile, SUBLANES, LANES)
        col_total = col_total.reshape(2, tile, SUBLANES, LANES)
        return row_total, col_total, cam_total

    depth = log_depth.reshape(2, SUBLANES, tile, LANES).transpose(0, 2, 1, 3)
    depth = relative(depth)
    col_depth = jnp.stack([exchange(depth[m], m) for m in range(2)])
    depths = spread(depth.reshape(-1, LANES), col_depth.reshape(-1, LANES))

    rates = [step_sizes[k : k + 1] for k in range(3)]
    camera_now, camera_state, camera_coef = update(
        camera_grads, 0, rates[1], camera.T, [], [], "cameras"
    )
    pair_now, pair_state, pair_coef = update(
        pair_grads, 0, rates[2], pair_pose.transpose(1, 2, 0), [], [], "pairs"
    )
    totals = None
    block_totals = []
    for step in range(1, ADAM_STEPS + 1):
        outs = grads_of_pairs(
            step,
            sizes,
            me,
            pair_coef,
            camera_coef,
            step_sizes,
            x,
            conf,
            table,
            (base, ray),
            depths,
            totals,
        )
        keep, send = outs[:2]
        col_parts = outs[2 : 2 + n_row]
        pair_sums, cam_sums = outs[2 + n_row :]
        row_total, col_total, cam_sums = reduce_blocks(keep, send, cam_sums, col_parts)
        if step < ADAM_STEPS:
            received = [
                exchange(jnp.stack([row_total[m], col_total[m]]), m) for m in range(2)
            ]
            total = row_total + jnp.stack([v[1] for v in received])
            col_total = col_total + jnp.stack([v[0] for v in received])
            message = jnp.concatenate([col_total.reshape(-1, LANES), cam_sums], axis=0)
            totals = spread(total.reshape(-1, LANES), message)
            cam_parts = totals[n_col:]
        else:
            received = [exchange(col_total[m], m) for m in range(2)]
            total = row_total + jnp.stack(received)
            others = [xor_permute(cam_sums, "row", e, n_row) for e in range(1, n_row)]
            cam_parts = [cam_sums, *others]
        block_totals.append(total)
        camera_now, camera_state, camera_coef = update(
            camera_grads, step, rates[1], camera_now, cam_parts, camera_state, "cameras"
        )
        pair_sums = jnp.sum(pair_sums, axis=-1).transpose(1, 2, 0)
        pair_now, pair_state, pair_coef = update(
            pair_grads, step, rates[2], pair_now, [pair_sums], pair_state, "pairs"
        )

    depth_now = depth
    depth_state = (jnp.zeros_like(depth),) * 2
    for step in range(1, ADAM_STEPS + 1):
        depth_now, *depth_state = adam_step(
            depth_now, block_totals[step - 1], *depth_state, step, step_sizes[0]
        )
    depth_now = relative(depth_now).transpose(0, 2, 1, 3).reshape(log_depth.shape)
    return depth_now, camera_now.T, pair_now.transpose(2, 0, 1)


def solution(mesh):
    n_row, n_col = mesh.shape["row"], mesh.shape["col"]
    in_specs = (
        P("row", "col", None, None, None),
        P("row", "col", None, None),
        P("row", "col", None),
        P("row", "col"),
        P(),
        P("row", "col", None),
        P(),
    )
    out_specs = (P("row", "col"), P(), P("row", "col", None))

    def body(pointmaps, *rest):
        rows, cols, pixels = pointmaps.shape[0], pointmaps.shape[1], pointmaps.shape[4]
        whole_tiles = pixels % (LANES * n_col) == 0 and (2 * pixels // LANES) % 16 == 0
        whole_tables = (rows * cols) % TABLE_PAIRS == 0
        paired = IMAGES <= LANES and rows == 2 * SUBLANES and cols == SUBLANES and n_col == 2 * n_row
        power = n_row & (n_row - 1) == 0
        if whole_tiles and whole_tables and paired and power:
            return fast_body(n_row, n_col, pointmaps, *rest)
        return general_body(pointmaps, *rest)

    return jax.shard_map(body, mesh=mesh, in_specs=in_specs, out_specs=out_specs, check_vma=False)
```

```python
import functools

import numpy as np

import jax
import jax.numpy as jnp
from jax import lax
from jax.experimental import pallas as pl
from jax.experimental.pallas import tpu as pltpu
from jax.sharding import PartitionSpec as P

IMAGES = 64
IMG_WIDTH = 224
IMG_HEIGHT = 224
WIN_ROWS = 64
ADAM_STEPS = 2

BETA_ONE = 0.9
BETA_TWO = 0.999
ADAM_EPS = 0.001
SOFTEN = 0.01

LANES = 128
SUBLANES = 8
TABLE_PAIRS = 64
WIDE = 2


def rotation(quaternion):
    length = jnp.sqrt(jnp.sum(quaternion * quaternion, axis=-1))
    w = quaternion[..., 0] / length
    x = quaternion[..., 1] / length
    y = quaternion[..., 2] / length
    z = quaternion[..., 3] / length
    return [
        [1.0 - 2.0 * (y * y + z * z), 2.0 * (x * y - w * z), 2.0 * (x * z + w * y)],
        [2.0 * (x * y + w * z), 1.0 - 2.0 * (x * x + z * z), 2.0 * (y * z - w * x)],
        [2.0 * (x * z - w * y), 2.0 * (y * z + w * x), 1.0 - 2.0 * (x * x + y * y)],
    ]


def adam_step(param, grad, first, second, step_number, step_size):
    first = BETA_ONE * first + (1.0 - BETA_ONE) * grad
    second = BETA_TWO * second + (1.0 - BETA_TWO) * grad * grad
    update = (
        step_size
        * (first / (1.0 - BETA_ONE**step_number))
        / (jnp.sqrt(second / (1.0 - BETA_TWO**step_number)) + ADAM_EPS)
    )
    return (param - update, first, second)


def world_points(log_depths, cameras):
    pixel_count = log_depths.shape[-1]
    position = jnp.arange(pixel_count, dtype=jnp.int32)
    across = (position % IMG_WIDTH).astype(jnp.float32) - (IMG_WIDTH - 1) / 2.0
    downward = (position // IMG_WIDTH + (IMG_HEIGHT - WIN_ROWS) // 2).astype(jnp.float32) - (
        IMG_HEIGHT - 1
    ) / 2.0
    focal_len = jnp.exp(cameras[:, 7:8])
    depth_map = jnp.exp(log_depths)
    ray_parts = (
        across[None, :] / focal_len * depth_map,
        downward[None, :] / focal_len * depth_map,
        depth_map,
    )
    turned = rotation(cameras[:, 0:4])
    return [
        turned[k][0][:, None] * ray_parts[0]
        + turned[k][1][:, None] * ray_parts[1]
        + turned[k][2][:, None] * ray_parts[2]
        + cameras[:, 4 + k][:, None]
        for k in range(3)
    ]


def pair_loss(
    first_depth,
    second_depth,
    first_camera,
    second_camera,
    pair_params,
    pointmaps,
    confidence,
    valid_blocks,
    first_ids,
    second_ids,
):
    first_world = world_points(first_depth, first_camera)
    second_world = world_points(second_depth, second_camera)
    pair_rotation = rotation(pair_params[..., 0:4])
    pair_scale = jnp.exp(pair_params[..., 7])
    pair_keep = (first_ids[:, None] != second_ids[None, :]).astype(jnp.float32)
    pixel_keep = (
        jnp.repeat(valid_blocks.astype(jnp.float32), IMG_WIDTH, axis=2) * pair_keep[:, :, None]
    )
    loss_sum = jnp.zeros((), jnp.float32)
    for side_index in range(2):
        if side_index == 0:
            points_side = [first_world[k][:, None, :] for k in range(3)]
        else:
            points_side = [second_world[k][None, :, :] for k in range(3)]
        source = [pointmaps[:, :, side_index, k, :].astype(jnp.float32) for k in range(3)]
        squared = SOFTEN
        for k in range(3):
            aligned = (
                pair_scale[..., None]
                * (
                    pair_rotation[k][0][..., None] * source[0]
                    + pair_rotation[k][1][..., None] * source[1]
                    + pair_rotation[k][2][..., None] * source[2]
                )
                + pair_params[..., 4 + k][..., None]
            )
            residual = points_side[k] - aligned
            squared = squared + residual * residual
        weight = confidence[:, :, side_index, :].astype(jnp.float32) * pixel_keep
        loss_sum = loss_sum + jnp.sum(weight * jnp.sqrt(squared))
    return loss_sum / (2.0 * (IMAGES - 1))


def general_body(pointmaps, confidence, valid_blocks, log_depth, camera, pair_pose, step_sizes):
    row_count = pointmaps.shape[0]
    col_count = pointmaps.shape[1]
    row_index = lax.axis_index("row")
    col_index = lax.axis_index("col")
    first_ids = row_index * row_count + jnp.arange(row_count, dtype=jnp.int32)
    second_ids = col_index * col_count + jnp.arange(col_count, dtype=jnp.int32)

    def local_loss(row_depth, col_depth, cameras, pair_params):
        first_camera = lax.dynamic_slice_in_dim(cameras, row_index * row_count, row_count, 0)
        second_camera = lax.dynamic_slice_in_dim(cameras, col_index * col_count, col_count, 0)
        return pair_loss(
            row_depth,
            col_depth,
            first_camera,
            second_camera,
            pair_params,
            pointmaps,
            confidence,
            valid_blocks,
            first_ids,
            second_ids,
        )

    depth_now, camera_now, pair_now = (log_depth, camera, pair_pose)
    depth_first = jnp.zeros_like(log_depth)
    depth_second = jnp.zeros_like(log_depth)
    camera_first = jnp.zeros_like(camera)
    camera_second = jnp.zeros_like(camera)
    pair_first = jnp.zeros_like(pair_pose)
    pair_second = jnp.zeros_like(pair_pose)
    for step_number in range(1, ADAM_STEPS + 1):
        row_depth = lax.all_gather(depth_now, "col", axis=1, tiled=True)
        every_image = lax.all_gather(depth_now, "row", axis=0, tiled=True)
        col_depth = lax.all_to_all(every_image, "col", split_axis=0, concat_axis=1, tiled=True)
        row_grad, col_grad, cam_grad, pair_grad = jax.grad(local_loss, argnums=(0, 1, 2, 3))(
            row_depth, col_depth, camera_now, pair_now
        )
        returned = lax.all_to_all(col_grad, "col", split_axis=1, concat_axis=0, tiled=True)
        from_cols = lax.psum_scatter(returned, "row", scatter_dimension=0, tiled=True)
        depth_grad = lax.psum_scatter(row_grad, "col", scatter_dimension=1, tiled=True)
        depth_grad = depth_grad + from_cols
        cam_total = lax.psum(cam_grad, ("row", "col"))
        depth_now, depth_first, depth_second = adam_step(
            depth_now, depth_grad, depth_first, depth_second, step_number, step_sizes[0]
        )
        camera_now, camera_first, camera_second = adam_step(
            camera_now, cam_total, camera_first, camera_second, step_number, step_sizes[1]
        )
        pair_now, pair_first, pair_second = adam_step(
            pair_now, pair_grad, pair_first, pair_second, step_number, step_sizes[2]
        )
    return (depth_now, camera_now, pair_now)


def pick_lanes(values, index):
    numbers = lax.GatherDimensionNumbers(
        offset_dims=(),
        collapsed_slice_dims=(1,),
        start_index_map=(1,),
        operand_batching_dims=(0,),
        start_indices_batching_dims=(0,),
    )
    return lax.gather(
        values,
        index[..., None],
        numbers,
        slice_sizes=(1, 1),
        mode=lax.GatherScatterMode.PROMISE_IN_BOUNDS,
    )


def cross(a, b):
    return [
        a[1] * b[2] - a[2] * b[1],
        a[2] * b[0] - a[0] * b[2],
        a[0] * b[1] - a[1] * b[0],
    ]


def grad_kernel(shape, step, *refs):
    rows, cols, slots, row_slots, tile = shape
    n_dep = slots + row_slots
    refs = list(refs)
    me, pair, cam, rate, x_ref, conf_ref, turn, spread, table, lane_base, ray = refs[:11]
    depth_refs = refs[11 : 11 + n_dep]
    at = 11 + n_dep
    grad_refs = None
    if step > 1:
        grad_refs = refs[at : at + n_dep]
        at += n_dep
    keep_out, send_out = refs[at : at + 2]
    col_out = refs[at + 2 : at + 2 + row_slots]
    at += 2 + row_slots
    pair_out, cam_out = refs[at : at + 2]
    chi_i, chi_j, grad_i, grad_j = refs[at + 2 :]

    i = pl.program_id(0)
    my_row, my_col = me[0], me[1]
    core = my_col & 1
    n_tiles = chi_i.shape[1]

    def depth_of(slot, start):
        take = pl.ds(start, tile, stride=SUBLANES)
        value = depth_refs[slot][take, :]
        if step > 1:
            g = grad_refs[slot][take, :]
            value = value - rate[0] * g / (jnp.abs(g) + ADAM_EPS)
        return jnp.exp(value)

    def put_points(dst, image, slot, start, block):
        depth = depth_of(slot, start)
        across = ray[0, block] / cam[12, image] * depth
        downward = ray[1, block] / cam[12, image] * depth
        for k in range(3):
            value = (
                cam[3 * k, image] * across
                + cam[3 * k + 1, image] * downward
                + cam[3 * k + 2, image] * depth
                + cam[9 + k, image]
            )
            dst[k, pl.ds(block * tile, tile), :] = value

    def finish(points, grads, image, block, sums):
        take = pl.ds(block * tile, tile)
        g = [grads[k, take, :] for k in range(3)]
        v = [points[k, take, :] - cam[9 + k, image] for k in range(3)]
        axis = [cam[3 * k + 2, image] for k in range(3)]
        by_depth = g[0] * v[0] + g[1] * v[1] + g[2] * v[2]
        depth = axis[0] * v[0] + axis[1] * v[1] + axis[2] * v[2]
        along = axis[0] * g[0] + axis[1] * g[1] + axis[2] * g[2]
        new = g + cross(v, g) + [by_depth - depth * along]
        return by_depth, [s + n for s, n in zip(sums, new)]

    def stack_sums(sums):
        parts = [jnp.sum(s, axis=0, keepdims=True) for s in sums]
        return jnp.concatenate(parts + [jnp.zeros((1, LANES), jnp.float32)], axis=0)

    def add_camera(image, sums):
        total = jnp.sum(stack_sums(sums), axis=1, keepdims=True)
        lane = lax.broadcasted_iota(jnp.int32, (SUBLANES, LANES), 1)
        cam_out[...] += jnp.where(lane == image, total, 0.0)

    def col_block(e, k_slot):
        return (my_row ^ e) * 2 + (k_slot ^ core)

    @pl.when(i == 0)
    def _():
        def one(j, carry):
            for e in range(row_slots):
                for k_slot in range(2):
                    put_points(
                        chi_j.at[j],
                        my_col * cols + j,
                        slots + e,
                        k_slot * tile * SUBLANES + j,
                        col_block(e, k_slot),
                    )
            return carry

        lax.fori_loop(0, cols, one, 0)
        grad_j[...] = jnp.zeros_like(grad_j)
        cam_out[...] = jnp.zeros_like(cam_out)

    t, m = i // SUBLANES, i % SUBLANES
    for d in range(slots):
        block = my_col ^ d
        t_slot = t ^ core ^ (d & 1)
        put_points(
            chi_i, my_row * rows + i, d, t_slot * tile * SUBLANES + m, block
        )
    grad_i[...] = jnp.zeros_like(grad_i)

    both = 2 * SUBLANES

    def one_pair(j, carry):
        q = i * cols + j
        shift = [pair[j, 9 + k, i] for k in range(3)]
        scale = pair[j, 12, i]
        which = q // TABLE_PAIRS
        lane_at = q % TABLE_PAIRS
        weights = [turn[0, j, pl.ds(k, 1), :] * spread[0] for k in range(3)]
        weights = jnp.concatenate(weights + [spread[1]], axis=0).astype(jnp.bfloat16)

        def one_chunk(ch, sums):
            sources = []
            for h in range(WIDE):
                packed = pl.ds(pl.multiple_of((WIDE * ch + h) * both, both), both)
                x = [x_ref[0, j, k, packed, :] for k in range(3)]
                sources.append(jnp.concatenate(x * 3 + [conf_ref[0, j, packed, :]], axis=0))
            source = jnp.concatenate(sources, axis=1)
            wide = jnp.dot(weights, source, preferred_element_type=jnp.float32)
            for h in range(WIDE):
                take = pl.ds(pl.multiple_of((WIDE * ch + h) * SUBLANES, SUBLANES), SUBLANES)
                turned = wide[:, h * LANES : (h + 1) * LANES]
                keep = pick_lanes(table[which, take, :], lane_base[take, :] + lane_at)
                for side, points, grads in (
                    (0, chi_i, grad_i),
                    (1, chi_j.at[j], grad_j.at[j]),
                ):
                    rows_of = [both * k + SUBLANES * side for k in range(4)]
                    y = [turned[a : a + SUBLANES] for a in rows_of[:3]]
                    weight = turned[rows_of[3] : rows_of[3] + SUBLANES] * keep
                    r = []
                    squared = SOFTEN
                    for k in range(3):
                        r.append(points[k, take, :] - (scale * y[k] + shift[k]))
                        squared = squared + r[k] * r[k]
                    scaled = weight * lax.rsqrt(squared)
                    g = [scaled * r[k] for k in range(3)]
                    for k in range(3):
                        grads[k, take, :] += g[k]
                    trace = g[0] * y[0] + g[1] * y[1] + g[2] * y[2]
                    new = g + cross(g, y) + [trace]
                    sums = tuple(s + n for s, n in zip(sums, new))
            return sums

        zero = jnp.zeros((SUBLANES, LANES), jnp.float32)
        sums = lax.fori_loop(0, n_tiles // (WIDE * SUBLANES), one_chunk, (zero,) * 7, unroll=True)
        pair_out[0, j] = stack_sums(sums)
        return carry

    lax.fori_loop(0, cols, one_pair, 0)

    zero = jnp.zeros((tile, LANES), jnp.float32)
    sums = [zero] * 7
    for d in range(slots):
        block = my_col ^ d
        t_slot = t ^ core ^ (d & 1)
        value, sums = finish(chi_i, grad_i, my_row * rows + i, block, sums)
        out = send_out if d & 1 else keep_out
        start = (d // 2) * (2 * tile * SUBLANES) + t_slot * tile * SUBLANES + m
        out[pl.ds(start, tile, stride=SUBLANES), :] = value
    add_camera(my_row * rows + i, sums)

    @pl.when(i == rows - 1)
    def _():
        def one(j, carry):
            sums = [zero] * 7
            for e in range(row_slots):
                for k_slot in range(2):
                    value, sums = finish(
                        chi_j.at[j], grad_j.at[j], my_col * cols + j, col_block(e, k_slot), sums
                    )
                    start = k_slot * tile * SUBLANES + j
                    col_out[e][pl.ds(start, tile, stride=SUBLANES), :] = value
            add_camera(my_col * cols + j, sums)
            return carry

        lax.fori_loop(0, cols, one, 0)


def grads_of_pairs(step, sizes, me, pair, cam, rate, x, conf, turn, consts, depths, totals):
    rows, cols, slots, row_slots, tile = sizes
    n_rows = 2 * slots * tile
    smem = pl.BlockSpec(memory_space=pltpu.SMEM)
    vmem = pl.BlockSpec(memory_space=pltpu.VMEM)
    operands = [me, pair, cam, rate, x, conf, turn, *consts, *depths]
    if step > 1:
        operands += totals
    in_specs = [smem] * 4 + [
        pl.BlockSpec((1, cols, 3, n_rows, LANES), lambda i: (i, 0, 0, 0, 0)),
        pl.BlockSpec((1, cols, n_rows, LANES), lambda i: (i, 0, 0, 0)),
        pl.BlockSpec((1, *turn.shape[1:]), lambda i: (i, 0, 0, 0)),
    ]
    in_specs += [vmem] * (len(operands) - len(in_specs))
    block = 2 * tile * SUBLANES
    f32 = jnp.float32
    out_shape = [
        jax.ShapeDtypeStruct((slots // 2 * block, LANES), f32),
        jax.ShapeDtypeStruct((slots // 2 * block, LANES), f32),
        *[jax.ShapeDtypeStruct((block, LANES), f32)] * row_slots,
        jax.ShapeDtypeStruct((rows, cols, SUBLANES, LANES), f32),
        jax.ShapeDtypeStruct((SUBLANES, LANES), f32),
    ]
    out_specs = [vmem] * (2 + row_slots) + [
        pl.BlockSpec((1, cols, SUBLANES, LANES), lambda i: (i, 0, 0, 0)),
        vmem,
    ]
    work = rows * cols * 3 * n_rows * LANES
    return pl.pallas_call(
        functools.partial(grad_kernel, sizes, step),
        grid=(rows,),
        in_specs=in_specs,
        out_specs=out_specs,
        out_shape=out_shape,
        scratch_shapes=[
            pltpu.VMEM((3, n_rows // 2, LANES), f32),
            pltpu.VMEM((cols, 3, n_rows // 2, LANES), f32),
            pltpu.VMEM((3, n_rows // 2, LANES), f32),
            pltpu.VMEM((cols, 3, n_rows // 2, LANES), f32),
        ],
        compiler_params=pltpu.CompilerParams(
            dimension_semantics=("arbitrary",), vmem_limit_bytes=52 * 1024 * 1024
        ),
        cost_estimate=pl.CostEstimate(
            flops=20 * work, bytes_accessed=3 * work, transcendentals=work // 3
        ),
        name=f"pair_grads_{step}",
    )(*operands)


def rotation_of(q):
    length = jnp.sqrt(q[0] * q[0] + q[1] * q[1] + q[2] * q[2] + q[3] * q[3])
    w, x, y, z = (part / length for part in q)
    return [
        1.0 - 2.0 * (y * y + z * z),
        2.0 * (x * y - w * z),
        2.0 * (x * z + w * y),
        2.0 * (x * y + w * z),
        1.0 - 2.0 * (x * x + z * z),
        2.0 * (y * z - w * x),
        2.0 * (x * z - w * y),
        2.0 * (y * z + w * x),
        1.0 - 2.0 * (x * x + y * y),
    ]


def quaternion_grad(q, torque):
    w, v = q[0], q[1:4]
    factor = 2.0 / (w * w + v[0] * v[0] + v[1] * v[1] + v[2] * v[2])
    c = cross(torque, v)
    real = -(torque[0] * v[0] + torque[1] * v[1] + torque[2] * v[2])
    return [factor * real] + [factor * (w * torque[k] + c[k]) for k in range(3)]


def pair_grads(p, s):
    scale = jnp.exp(p[7])
    parts = quaternion_grad(p, [scale * s[k] for k in (3, 4, 5)])
    return parts + [-s[0], -s[1], -s[2], -scale * s[6]]


def camera_grads(p, s):
    return quaternion_grad(p, s[3:6]) + [s[0], s[1], s[2], -s[6]]


def update_kernel(grads_of, step, n_sums, axes, *refs):
    refs = list(refs)
    rate, params = refs[:2]

    def at(ref, k):
        return ref.at[:, k, :] if axes == 3 else ref.at[pl.ds(k, 1), :]

    p = [at(params, k)[...] for k in range(8)]
    rest = refs[2:]
    if step:
        width = p[0].shape[-1]
        parts = []
        for sums in rest[:n_sums]:
            top = sums.shape[-2] - SUBLANES
            if axes == 3:
                parts.append([sums[:, k, :] for k in range(7)])
            else:
                parts.append([sums[pl.ds(top + k, 1), pl.ds(0, width)] for k in range(7)])
        total = [tree_sum([part[k] for part in parts]) for k in range(7)]
        g = grads_of(p, total)
        rest = rest[n_sums:]
        first, second = [jnp.zeros_like(v) for v in p], [jnp.zeros_like(v) for v in p]
        if step > 1:
            first = [at(rest[0], k)[...] for k in range(8)]
            second = [at(rest[1], k)[...] for k in range(8)]
            rest = rest[2:]
        for k in range(8):
            p[k], first[k], second[k] = adam_step(p[k], g[k], first[k], second[k], step, rate[0])
            at(rest[0], k)[...] = p[k]
            if step < ADAM_STEPS:
                at(rest[1], k)[...] = first[k]
                at(rest[2], k)[...] = second[k]
        rest = rest[3:] if step < ADAM_STEPS else rest[1:]
    if step < ADAM_STEPS:
        values = rotation_of(p[0:4]) + p[4:7] + [jnp.exp(p[7])]
        for k, value in enumerate(values):
            at(rest[0], k)[...] = value


def update(grads_of, step, rate, params, sums, state, name):
    f32 = jnp.float32
    like = jax.ShapeDtypeStruct(params.shape, f32)
    coef_shape = (*params.shape[:-2], 16, params.shape[-1])
    out_shape = []
    if step:
        out_shape += [like] * (3 if step < ADAM_STEPS else 1)
    if step < ADAM_STEPS:
        out_shape.append(jax.ShapeDtypeStruct(coef_shape, f32))
    vmem = pl.BlockSpec(memory_space=pltpu.VMEM)
    operands = [params, *sums, *(state if step > 1 else [])]
    outs = pl.pallas_call(
        functools.partial(update_kernel, grads_of, step, len(sums), params.ndim),
        in_specs=[pl.BlockSpec(memory_space=pltpu.SMEM)] + [vmem] * len(operands),
        out_specs=[vmem] * len(out_shape),
        out_shape=out_shape,
        compiler_params=pltpu.CompilerParams(vmem_limit_bytes=4 * 1024 * 1024),
        cost_estimate=pl.CostEstimate(flops=10000, bytes_accessed=100000, transcendentals=0),
        name=f"{name}_{step}",
    )(rate, *operands)
    if not step:
        return params, [], outs[0]
    if step < ADAM_STEPS:
        return outs[0], outs[1:3], outs[3]
    return outs[0], [], None


def pixel_constants(n_tiles, blocks):
    pixel = np.arange(n_tiles * LANES).reshape(n_tiles, LANES)
    line = pixel // IMG_WIDTH
    across = (pixel % IMG_WIDTH).astype(np.float32) - np.float32((IMG_WIDTH - 1) / 2.0)
    downward = (line + (IMG_HEIGHT - WIN_ROWS) // 2).astype(np.float32) - np.float32(
        (IMG_HEIGHT - 1) / 2.0
    )
    ray = np.stack([across, downward]).reshape(2, blocks, n_tiles // blocks, LANES)
    first = line[:, 0]
    base = (line != first[:, None]).astype(np.int32) * TABLE_PAIRS
    lines = np.stack([first, np.minimum(first + 1, WIN_ROWS - 1)])
    pick = (lines[:, :, None] == np.arange(WIN_ROWS)).astype(np.float32)
    return jnp.asarray(base), jnp.asarray(ray), pick


def spread_of_rows():
    both = 2 * SUBLANES
    row = np.arange(both)
    source = 2 * (row % SUBLANES) + row // SUBLANES
    one = (source[:, None] == row[None, :]).astype(np.float32)
    points = np.concatenate([np.tile(one, 9), np.zeros_like(one)], axis=1)
    confidence = np.concatenate([np.zeros((both, 9 * both), np.float32), one], axis=1)
    return jnp.asarray(np.stack([points, confidence]))


def turning_weights(coef):
    entries = coef.transpose(2, 0, 1)[:, :, :9].reshape(coef.shape[2], coef.shape[0], 3, 1, 3)
    high = lax.reduce_precision(entries, 8, 7)
    middle = lax.reduce_precision(entries - high, 8, 7)
    low = lax.reduce_precision(entries - high - middle, 8, 7)
    parts = jnp.concatenate([high, middle, low], axis=3).reshape(*entries.shape[:3], 9)
    over = np.repeat(np.eye(9, 10, dtype=np.float32), 2 * SUBLANES, axis=1)
    return lax.dot_general(parts, jnp.asarray(over), (((3,), (0,)), ((), ())))


def tree_sum(parts):
    while len(parts) > 1:
        parts = [a + b for a, b in zip(parts[::2], parts[1::2])]
    return parts[0]


def xor_permute(value, axis, bit, size):
    return lax.ppermute(value, axis, [(c, c ^ bit) for c in range(size)])


def fast_body(n_row, n_col, pointmaps, confidence, valid_blocks, log_depth, camera, pair_pose, step_sizes):
    rows, cols = pointmaps.shape[:2]
    pixels = pointmaps.shape[4]
    n_tiles = pixels // LANES
    tile = n_tiles // n_col
    sizes = (rows, cols, n_col, n_row, tile)
    row_index = lax.axis_index("row")
    col_index = lax.axis_index("col")
    core = col_index % 2
    me = jnp.stack([row_index, col_index]).astype(jnp.int32)
    f32 = jnp.float32

    x = pointmaps.transpose(0, 1, 3, 2, 4).reshape(rows, cols, 3, 2, n_tiles, LANES)
    x = x.transpose(0, 1, 2, 4, 3, 5).reshape(rows, cols, 3, 2 * n_tiles, LANES)
    conf = confidence.reshape(rows, cols, 2, n_tiles, LANES)
    conf = conf.transpose(0, 1, 3, 2, 4).reshape(rows, cols, 2 * n_tiles, LANES)

    base, ray, pick = pixel_constants(n_tiles, n_col)
    first_ids = row_index * rows + jnp.arange(rows, dtype=jnp.int32)
    second_ids = col_index * cols + jnp.arange(cols, dtype=jnp.int32)
    different = (first_ids[:, None] != second_ids[None, :]).astype(f32)
    share = different / (2.0 * (IMAGES - 1))
    valid = (valid_blocks.astype(f32)).reshape(rows * cols, WIN_ROWS)
    picked = lax.dot_general(
        jnp.asarray(pick.reshape(-1, WIN_ROWS)), valid, (((1,), (1,)), ((), ()))
    )
    picked = picked * share.reshape(1, rows * cols)
    picked = picked.reshape(2, n_tiles, rows * cols // TABLE_PAIRS, TABLE_PAIRS)
    table = picked.transpose(2, 1, 0, 3).reshape(-1, n_tiles, 2 * TABLE_PAIRS)

    def relative(value):
        return jnp.where(core == 0, value, value[::-1])

    def swap_perm(m):
        pairs = []
        for r in range(n_row):
            for c in range(n_col):
                to = (c // 2) * n_col + 2 * r + (m ^ (c & 1))
                pairs.append((r * n_col + c, to))
        return pairs

    def exchange(value, m):
        return lax.ppermute(value, ("row", "col"), swap_perm(m))

    def spread(row_part, col_part):
        own, other, down = [row_part], [], [col_part]
        for d in range(1, n_col // 2):
            own.append(xor_permute(row_part, "col", 2 * d, n_col))
        for e in range(1, n_row):
            down.append(xor_permute(col_part, "row", e, n_row))
        for d in range(n_col // 2):
            other.append(xor_permute(own[d], "col", 1, n_col))
        flat = []
        for d in range(n_col // 2):
            flat += [own[d], other[d]]
        return flat + down

    block = 2 * tile * SUBLANES

    def reduce_blocks(keep, send, cam, col_parts):
        got = xor_permute(send, "col", 1, n_col)
        cam = cam + xor_permute(cam, "col", 1, n_col)
        total = (keep + got).reshape(n_col // 2, block, LANES)
        col_total = col_parts[0]
        for e in range(1, n_row):
            col_total = col_total + xor_permute(col_parts[e], "row", e, n_row)
        row_total, cams = total[0], [cam]
        for d in range(1, n_col // 2):
            message = jnp.concatenate([total[d], cam], axis=0)
            message = xor_permute(message, "col", 2 * d, n_col)
            row_total = row_total + message[:block]
            cams.append(message[block:])
        cam_total = tree_sum(cams)
        row_total = row_total.reshape(2, tile, SUBLANES, LANES)
        col_total = col_total.reshape(2, tile, SUBLANES, LANES)
        return row_total, col_total, cam_total

    depth = log_depth.reshape(2, SUBLANES, tile, LANES).transpose(0, 2, 1, 3)
    depth = relative(depth)
    col_depth = jnp.stack([exchange(depth[m], m) for m in range(2)])
    depths = spread(depth.reshape(-1, LANES), col_depth.reshape(-1, LANES))

    rates = [step_sizes[k : k + 1] for k in range(3)]
    camera_now, camera_state, camera_coef = update(
        camera_grads, 0, rates[1], camera.T, [], [], "cameras"
    )
    pair_now, pair_state, pair_coef = update(
        pair_grads, 0, rates[2], pair_pose.transpose(1, 2, 0), [], [], "pairs"
    )
    totals = None
    block_totals = []
    for step in range(1, ADAM_STEPS + 1):
        outs = grads_of_pairs(
            step,
            sizes,
            me,
            pair_coef,
            camera_coef,
            step_sizes,
            x,
            conf,
            turning_weights(pair_coef),
            (spread_of_rows(), table, base, ray),
            depths,
            totals,
        )
        keep, send = outs[:2]
        col_parts = outs[2 : 2 + n_row]
        pair_sums, cam_sums = outs[2 + n_row :]
        row_total, col_total, cam_sums = reduce_blocks(keep, send, cam_sums, col_parts)
        if step < ADAM_STEPS:
            received = [
                exchange(jnp.stack([row_total[m], col_total[m]]), m) for m in range(2)
            ]
            total = row_total + jnp.stack([v[1] for v in received])
            col_total = col_total + jnp.stack([v[0] for v in received])
            message = jnp.concatenate([col_total.reshape(-1, LANES), cam_sums], axis=0)
            totals = spread(total.reshape(-1, LANES), message)
            cam_parts = totals[n_col:]
        else:
            received = [exchange(col_total[m], m) for m in range(2)]
            total = row_total + jnp.stack(received)
            others = [xor_permute(cam_sums, "row", e, n_row) for e in range(1, n_row)]
            cam_parts = [cam_sums, *others]
        block_totals.append(total)
        camera_now, camera_state, camera_coef = update(
            camera_grads, step, rates[1], camera_now, cam_parts, camera_state, "cameras"
        )
        pair_sums = jnp.sum(pair_sums, axis=-1).transpose(1, 2, 0)
        pair_now, pair_state, pair_coef = update(
            pair_grads, step, rates[2], pair_now, [pair_sums], pair_state, "pairs"
        )

    depth_now = depth
    depth_state = (jnp.zeros_like(depth),) * 2
    for step in range(1, ADAM_STEPS + 1):
        depth_now, *depth_state = adam_step(
            depth_now, block_totals[step - 1], *depth_state, step, step_sizes[0]
        )
    depth_now = relative(depth_now).transpose(0, 2, 1, 3).reshape(log_depth.shape)
    return depth_now, camera_now.T, pair_now.transpose(2, 0, 1)


def solution(mesh):
    n_row, n_col = mesh.shape["row"], mesh.shape["col"]
    in_specs = (
        P("row", "col", None, None, None),
        P("row", "col", None, None),
        P("row", "col", None),
        P("row", "col"),
        P(),
        P("row", "col", None),
        P(),
    )
    out_specs = (P("row", "col"), P(), P("row", "col", None))

    def body(pointmaps, *rest):
        rows, cols, pixels = pointmaps.shape[0], pointmaps.shape[1], pointmaps.shape[4]
        whole_tiles = pixels % (LANES * n_col) == 0 and (pixels // LANES) % (WIDE * SUBLANES) == 0
        whole_tables = (rows * cols) % TABLE_PAIRS == 0
        paired = IMAGES <= LANES and rows == 2 * SUBLANES and cols == SUBLANES and n_col == 2 * n_row
        power = n_row & (n_row - 1) == 0
        if whole_tiles and whole_tables and paired and power:
            return fast_body(n_row, n_col, pointmaps, *rest)
        return general_body(pointmaps, *rest)

    return jax.shard_map(body, mesh=mesh, in_specs=in_specs, out_specs=out_specs, check_vma=False)
```

```python
import functools

import numpy as np

import jax
import jax.numpy as jnp
from jax import lax
from jax.experimental import pallas as pl
from jax.experimental.pallas import tpu as pltpu
from jax.sharding import PartitionSpec as P

IMAGES = 64
IMG_WIDTH = 224
IMG_HEIGHT = 224
WIN_ROWS = 64
ADAM_STEPS = 2

BETA_ONE = 0.9
BETA_TWO = 0.999
ADAM_EPS = 0.001
SOFTEN = 0.01

LANES = 128
SUBLANES = 8
TABLE_PAIRS = 64


def rotation(quaternion):
    length = jnp.sqrt(jnp.sum(quaternion * quaternion, axis=-1))
    w = quaternion[..., 0] / length
    x = quaternion[..., 1] / length
    y = quaternion[..., 2] / length
    z = quaternion[..., 3] / length
    return [
        [1.0 - 2.0 * (y * y + z * z), 2.0 * (x * y - w * z), 2.0 * (x * z + w * y)],
        [2.0 * (x * y + w * z), 1.0 - 2.0 * (x * x + z * z), 2.0 * (y * z - w * x)],
        [2.0 * (x * z - w * y), 2.0 * (y * z + w * x), 1.0 - 2.0 * (x * x + y * y)],
    ]


def adam_step(param, grad, first, second, step_number, step_size):
    first = BETA_ONE * first + (1.0 - BETA_ONE) * grad
    second = BETA_TWO * second + (1.0 - BETA_TWO) * grad * grad
    update = (
        step_size
        * (first / (1.0 - BETA_ONE**step_number))
        / (jnp.sqrt(second / (1.0 - BETA_TWO**step_number)) + ADAM_EPS)
    )
    return (param - update, first, second)


def world_points(log_depths, cameras):
    pixel_count = log_depths.shape[-1]
    position = jnp.arange(pixel_count, dtype=jnp.int32)
    across = (position % IMG_WIDTH).astype(jnp.float32) - (IMG_WIDTH - 1) / 2.0
    downward = (position // IMG_WIDTH + (IMG_HEIGHT - WIN_ROWS) // 2).astype(jnp.float32) - (
        IMG_HEIGHT - 1
    ) / 2.0
    focal_len = jnp.exp(cameras[:, 7:8])
    depth_map = jnp.exp(log_depths)
    ray_parts = (
        across[None, :] / focal_len * depth_map,
        downward[None, :] / focal_len * depth_map,
        depth_map,
    )
    turned = rotation(cameras[:, 0:4])
    return [
        turned[k][0][:, None] * ray_parts[0]
        + turned[k][1][:, None] * ray_parts[1]
        + turned[k][2][:, None] * ray_parts[2]
        + cameras[:, 4 + k][:, None]
        for k in range(3)
    ]


def pair_loss(
    first_depth,
    second_depth,
    first_camera,
    second_camera,
    pair_params,
    pointmaps,
    confidence,
    valid_blocks,
    first_ids,
    second_ids,
):
    first_world = world_points(first_depth, first_camera)
    second_world = world_points(second_depth, second_camera)
    pair_rotation = rotation(pair_params[..., 0:4])
    pair_scale = jnp.exp(pair_params[..., 7])
    pair_keep = (first_ids[:, None] != second_ids[None, :]).astype(jnp.float32)
    pixel_keep = (
        jnp.repeat(valid_blocks.astype(jnp.float32), IMG_WIDTH, axis=2) * pair_keep[:, :, None]
    )
    loss_sum = jnp.zeros((), jnp.float32)
    for side_index in range(2):
        if side_index == 0:
            points_side = [first_world[k][:, None, :] for k in range(3)]
        else:
            points_side = [second_world[k][None, :, :] for k in range(3)]
        source = [pointmaps[:, :, side_index, k, :].astype(jnp.float32) for k in range(3)]
        squared = SOFTEN
        for k in range(3):
            aligned = (
                pair_scale[..., None]
                * (
                    pair_rotation[k][0][..., None] * source[0]
                    + pair_rotation[k][1][..., None] * source[1]
                    + pair_rotation[k][2][..., None] * source[2]
                )
                + pair_params[..., 4 + k][..., None]
            )
            residual = points_side[k] - aligned
            squared = squared + residual * residual
        weight = confidence[:, :, side_index, :].astype(jnp.float32) * pixel_keep
        loss_sum = loss_sum + jnp.sum(weight * jnp.sqrt(squared))
    return loss_sum / (2.0 * (IMAGES - 1))


def general_body(pointmaps, confidence, valid_blocks, log_depth, camera, pair_pose, step_sizes):
    row_count = pointmaps.shape[0]
    col_count = pointmaps.shape[1]
    row_index = lax.axis_index("row")
    col_index = lax.axis_index("col")
    first_ids = row_index * row_count + jnp.arange(row_count, dtype=jnp.int32)
    second_ids = col_index * col_count + jnp.arange(col_count, dtype=jnp.int32)

    def local_loss(row_depth, col_depth, cameras, pair_params):
        first_camera = lax.dynamic_slice_in_dim(cameras, row_index * row_count, row_count, 0)
        second_camera = lax.dynamic_slice_in_dim(cameras, col_index * col_count, col_count, 0)
        return pair_loss(
            row_depth,
            col_depth,
            first_camera,
            second_camera,
            pair_params,
            pointmaps,
            confidence,
            valid_blocks,
            first_ids,
            second_ids,
        )

    depth_now, camera_now, pair_now = (log_depth, camera, pair_pose)
    depth_first = jnp.zeros_like(log_depth)
    depth_second = jnp.zeros_like(log_depth)
    camera_first = jnp.zeros_like(camera)
    camera_second = jnp.zeros_like(camera)
    pair_first = jnp.zeros_like(pair_pose)
    pair_second = jnp.zeros_like(pair_pose)
    for step_number in range(1, ADAM_STEPS + 1):
        row_depth = lax.all_gather(depth_now, "col", axis=1, tiled=True)
        every_image = lax.all_gather(depth_now, "row", axis=0, tiled=True)
        col_depth = lax.all_to_all(every_image, "col", split_axis=0, concat_axis=1, tiled=True)
        row_grad, col_grad, cam_grad, pair_grad = jax.grad(local_loss, argnums=(0, 1, 2, 3))(
            row_depth, col_depth, camera_now, pair_now
        )
        returned = lax.all_to_all(col_grad, "col", split_axis=1, concat_axis=0, tiled=True)
        from_cols = lax.psum_scatter(returned, "row", scatter_dimension=0, tiled=True)
        depth_grad = lax.psum_scatter(row_grad, "col", scatter_dimension=1, tiled=True)
        depth_grad = depth_grad + from_cols
        cam_total = lax.psum(cam_grad, ("row", "col"))
        depth_now, depth_first, depth_second = adam_step(
            depth_now, depth_grad, depth_first, depth_second, step_number, step_sizes[0]
        )
        camera_now, camera_first, camera_second = adam_step(
            camera_now, cam_total, camera_first, camera_second, step_number, step_sizes[1]
        )
        pair_now, pair_first, pair_second = adam_step(
            pair_now, pair_grad, pair_first, pair_second, step_number, step_sizes[2]
        )
    return (depth_now, camera_now, pair_now)


def pick_lanes(values, index):
    numbers = lax.GatherDimensionNumbers(
        offset_dims=(),
        collapsed_slice_dims=(1,),
        start_index_map=(1,),
        operand_batching_dims=(0,),
        start_indices_batching_dims=(0,),
    )
    return lax.gather(
        values,
        index[..., None],
        numbers,
        slice_sizes=(1, 1),
        mode=lax.GatherScatterMode.PROMISE_IN_BOUNDS,
    )


def cross(a, b):
    return [
        a[1] * b[2] - a[2] * b[1],
        a[2] * b[0] - a[0] * b[2],
        a[0] * b[1] - a[1] * b[0],
    ]


def grad_kernel(shape, step, *refs):
    rows, cols, slots, row_slots, tile = shape
    n_dep = slots + row_slots
    refs = list(refs)
    me, pair, cam, rate, x_ref, conf_ref, table, lane_base, ray = refs[:9]
    depth_refs = refs[9 : 9 + n_dep]
    at = 9 + n_dep
    grad_refs = None
    if step > 1:
        grad_refs = refs[at : at + n_dep]
        at += n_dep
    keep_out, send_out = refs[at : at + 2]
    col_out = refs[at + 2 : at + 2 + row_slots]
    at += 2 + row_slots
    pair_out, cam_out = refs[at : at + 2]
    chi_i, chi_j, grad_i, grad_j, wide = refs[at + 2 :]

    i = pl.program_id(0)
    my_row, my_col = me[0], me[1]
    core = my_col & 1
    n_tiles = chi_i.shape[1]

    def depth_of(slot, start):
        take = pl.ds(start, tile, stride=SUBLANES)
        value = depth_refs[slot][take, :]
        if step > 1:
            g = grad_refs[slot][take, :]
            value = value - rate[0] * g / (jnp.abs(g) + ADAM_EPS)
        return jnp.exp(value)

    def put_points(dst, image, slot, start, block):
        depth = depth_of(slot, start)
        across = ray[0, block] / cam[12, image] * depth
        downward = ray[1, block] / cam[12, image] * depth
        for k in range(3):
            value = (
                cam[3 * k, image] * across
                + cam[3 * k + 1, image] * downward
                + cam[3 * k + 2, image] * depth
                + cam[9 + k, image]
            )
            dst[k, pl.ds(block * tile, tile), :] = value

    def finish(points, grads, image, block, sums):
        take = pl.ds(block * tile, tile)
        g = [grads[k, take, :] for k in range(3)]
        v = [points[k, take, :] - cam[9 + k, image] for k in range(3)]
        axis = [cam[3 * k + 2, image] for k in range(3)]
        by_depth = g[0] * v[0] + g[1] * v[1] + g[2] * v[2]
        depth = axis[0] * v[0] + axis[1] * v[1] + axis[2] * v[2]
        along = axis[0] * g[0] + axis[1] * g[1] + axis[2] * g[2]
        new = g + cross(v, g) + [by_depth - depth * along]
        return by_depth, [s + n for s, n in zip(sums, new)]

    def stack_sums(sums):
        parts = [jnp.sum(s, axis=0, keepdims=True) for s in sums]
        return jnp.concatenate(parts + [jnp.zeros((1, LANES), jnp.float32)], axis=0)

    def add_camera(image, sums):
        total = jnp.sum(stack_sums(sums), axis=1, keepdims=True)
        lane = lax.broadcasted_iota(jnp.int32, (SUBLANES, LANES), 1)
        cam_out[...] += jnp.where(lane == image, total, 0.0)

    def col_block(e, k_slot):
        return (my_row ^ e) * 2 + (k_slot ^ core)

    @pl.when(i == 0)
    def _():
        def one(j, carry):
            for e in range(row_slots):
                for k_slot in range(2):
                    put_points(
                        chi_j.at[j],
                        my_col * cols + j,
                        slots + e,
                        k_slot * tile * SUBLANES + j,
                        col_block(e, k_slot),
                    )
            return carry

        lax.fori_loop(0, cols, one, 0)
        grad_j[...] = jnp.zeros_like(grad_j)
        cam_out[...] = jnp.zeros_like(cam_out)

    t, m = i // SUBLANES, i % SUBLANES
    for d in range(slots):
        block = my_col ^ d
        t_slot = t ^ core ^ (d & 1)
        put_points(
            chi_i, my_row * rows + i, d, t_slot * tile * SUBLANES + m, block
        )
    grad_i[...] = jnp.zeros_like(grad_i)

    both = 2 * SUBLANES

    def one_pair(j, carry):
        q = i * cols + j
        shift = [pair[j, 9 + k, i] for k in range(3)]
        scale = pair[j, 12, i]
        which = q // TABLE_PAIRS
        lane_at = q % TABLE_PAIRS
        turn = [pair[j, n, i] for n in range(9)]

        def one_chunk(ch, sums):
            packed = pl.ds(pl.multiple_of(ch * both, both), both)
            take = pl.ds(pl.multiple_of(ch * SUBLANES, SUBLANES), SUBLANES)
            for k in range(3):
                wide[k, packed, :] = x_ref[0, j, k, packed, :].astype(jnp.float32)
            wide[3, packed, :] = conf_ref[0, j, packed, :].astype(jnp.float32)
            keep = pick_lanes(table[which, take, :], lane_base[take, :] + lane_at)
            for side, points, grads in ((0, chi_i, grad_i), (1, chi_j.at[j], grad_j.at[j])):
                alternate = pl.ds(ch * both + side, SUBLANES, stride=2)
                x = [wide[k, alternate, :] for k in range(3)]
                weight = wide[3, alternate, :] * keep
                y, r = [], []
                squared = SOFTEN
                for k in range(3):
                    y.append(
                        turn[3 * k] * x[0] + turn[3 * k + 1] * x[1] + turn[3 * k + 2] * x[2]
                    )
                    r.append(points[k, take, :] - (scale * y[k] + shift[k]))
                    squared = squared + r[k] * r[k]
                scaled = weight * lax.rsqrt(squared)
                g = [scaled * r[k] for k in range(3)]
                for k in range(3):
                    grads[k, take, :] += g[k]
                trace = g[0] * y[0] + g[1] * y[1] + g[2] * y[2]
                new = g + cross(g, y) + [trace]
                sums = tuple(s + n for s, n in zip(sums, new))
            return sums

        zero = jnp.zeros((SUBLANES, LANES), jnp.float32)
        sums = lax.fori_loop(0, n_tiles // SUBLANES, one_chunk, (zero,) * 7, unroll=True)
        pair_out[0, j] = stack_sums(sums)
        return carry

    lax.fori_loop(0, cols, one_pair, 0)

    zero = jnp.zeros((tile, LANES), jnp.float32)
    sums = [zero] * 7
    for d in range(slots):
        block = my_col ^ d
        t_slot = t ^ core ^ (d & 1)
        value, sums = finish(chi_i, grad_i, my_row * rows + i, block, sums)
        out = send_out if d & 1 else keep_out
        start = (d // 2) * (2 * tile * SUBLANES) + t_slot * tile * SUBLANES + m
        out[pl.ds(start, tile, stride=SUBLANES), :] = value
    add_camera(my_row * rows + i, sums)

    @pl.when(i == rows - 1)
    def _():
        def one(j, carry):
            sums = [zero] * 7
            for e in range(row_slots):
                for k_slot in range(2):
                    value, sums = finish(
                        chi_j.at[j], grad_j.at[j], my_col * cols + j, col_block(e, k_slot), sums
                    )
                    start = k_slot * tile * SUBLANES + j
                    col_out[e][pl.ds(start, tile, stride=SUBLANES), :] = value
            add_camera(my_col * cols + j, sums)
            return carry

        lax.fori_loop(0, cols, one, 0)


def grads_of_pairs(step, sizes, me, pair, cam, rate, x, conf, table, consts, depths, totals):
    rows, cols, slots, row_slots, tile = sizes
    n_rows = 2 * slots * tile
    smem = pl.BlockSpec(memory_space=pltpu.SMEM)
    vmem = pl.BlockSpec(memory_space=pltpu.VMEM)
    operands = [me, pair, cam, rate, x, conf, table, *consts, *depths]
    if step > 1:
        operands += totals
    in_specs = [smem] * 4 + [
        pl.BlockSpec((1, cols, 3, n_rows, LANES), lambda i: (i, 0, 0, 0, 0)),
        pl.BlockSpec((1, cols, n_rows, LANES), lambda i: (i, 0, 0, 0)),
    ]
    in_specs += [vmem] * (len(operands) - len(in_specs))
    block = 2 * tile * SUBLANES
    f32 = jnp.float32
    out_shape = [
        jax.ShapeDtypeStruct((slots // 2 * block, LANES), f32),
        jax.ShapeDtypeStruct((slots // 2 * block, LANES), f32),
        *[jax.ShapeDtypeStruct((block, LANES), f32)] * row_slots,
        jax.ShapeDtypeStruct((rows, cols, SUBLANES, LANES), f32),
        jax.ShapeDtypeStruct((SUBLANES, LANES), f32),
    ]
    out_specs = [vmem] * (2 + row_slots) + [
        pl.BlockSpec((1, cols, SUBLANES, LANES), lambda i: (i, 0, 0, 0)),
        vmem,
    ]
    work = rows * cols * 3 * n_rows * LANES
    return pl.pallas_call(
        functools.partial(grad_kernel, sizes, step),
        grid=(rows,),
        in_specs=in_specs,
        out_specs=out_specs,
        out_shape=out_shape,
        scratch_shapes=[
            pltpu.VMEM((3, n_rows // 2, LANES), f32),
            pltpu.VMEM((cols, 3, n_rows // 2, LANES), f32),
            pltpu.VMEM((3, n_rows // 2, LANES), f32),
            pltpu.VMEM((cols, 3, n_rows // 2, LANES), f32),
            pltpu.VMEM((4, n_rows, LANES), f32),
        ],
        compiler_params=pltpu.CompilerParams(
            dimension_semantics=("arbitrary",), vmem_limit_bytes=52 * 1024 * 1024
        ),
        cost_estimate=pl.CostEstimate(
            flops=20 * work, bytes_accessed=3 * work, transcendentals=work // 3
        ),
        name=f"pair_grads_{step}",
    )(*operands)


def rotation_of(q):
    length = jnp.sqrt(q[0] * q[0] + q[1] * q[1] + q[2] * q[2] + q[3] * q[3])
    w, x, y, z = (part / length for part in q)
    return [
        1.0 - 2.0 * (y * y + z * z),
        2.0 * (x * y - w * z),
        2.0 * (x * z + w * y),
        2.0 * (x * y + w * z),
        1.0 - 2.0 * (x * x + z * z),
        2.0 * (y * z - w * x),
        2.0 * (x * z - w * y),
        2.0 * (y * z + w * x),
        1.0 - 2.0 * (x * x + y * y),
    ]


def quaternion_grad(q, torque):
    w, v = q[0], q[1:4]
    factor = 2.0 / (w * w + v[0] * v[0] + v[1] * v[1] + v[2] * v[2])
    c = cross(torque, v)
    real = -(torque[0] * v[0] + torque[1] * v[1] + torque[2] * v[2])
    return [factor * real] + [factor * (w * torque[k] + c[k]) for k in range(3)]


def pair_grads(p, s):
    scale = jnp.exp(p[7])
    parts = quaternion_grad(p, [scale * s[k] for k in (3, 4, 5)])
    return parts + [-s[0], -s[1], -s[2], -scale * s[6]]


def camera_grads(p, s):
    return quaternion_grad(p, s[3:6]) + [s[0], s[1], s[2], -s[6]]


def update_kernel(grads_of, step, n_sums, axes, *refs):
    refs = list(refs)
    rate, params = refs[:2]

    def at(ref, k):
        return ref.at[:, k, :] if axes == 3 else ref.at[pl.ds(k, 1), :]

    p = [at(params, k)[...] for k in range(8)]
    rest = refs[2:]
    if step:
        width = p[0].shape[-1]
        parts = []
        for sums in rest[:n_sums]:
            top = sums.shape[-2] - SUBLANES
            if axes == 3:
                parts.append([sums[:, k, :] for k in range(7)])
            else:
                parts.append([sums[pl.ds(top + k, 1), pl.ds(0, width)] for k in range(7)])
        total = [tree_sum([part[k] for part in parts]) for k in range(7)]
        g = grads_of(p, total)
        rest = rest[n_sums:]
        first, second = [jnp.zeros_like(v) for v in p], [jnp.zeros_like(v) for v in p]
        if step > 1:
            first = [at(rest[0], k)[...] for k in range(8)]
            second = [at(rest[1], k)[...] for k in range(8)]
            rest = rest[2:]
        for k in range(8):
            p[k], first[k], second[k] = adam_step(p[k], g[k], first[k], second[k], step, rate[0])
            at(rest[0], k)[...] = p[k]
            if step < ADAM_STEPS:
                at(rest[1], k)[...] = first[k]
                at(rest[2], k)[...] = second[k]
        rest = rest[3:] if step < ADAM_STEPS else rest[1:]
    if step < ADAM_STEPS:
        values = rotation_of(p[0:4]) + p[4:7] + [jnp.exp(p[7])]
        for k, value in enumerate(values):
            at(rest[0], k)[...] = value


def update(grads_of, step, rate, params, sums, state, name):
    f32 = jnp.float32
    like = jax.ShapeDtypeStruct(params.shape, f32)
    coef_shape = (*params.shape[:-2], 16, params.shape[-1])
    out_shape = []
    if step:
        out_shape += [like] * (3 if step < ADAM_STEPS else 1)
    if step < ADAM_STEPS:
        out_shape.append(jax.ShapeDtypeStruct(coef_shape, f32))
    vmem = pl.BlockSpec(memory_space=pltpu.VMEM)
    operands = [params, *sums, *(state if step > 1 else [])]
    outs = pl.pallas_call(
        functools.partial(update_kernel, grads_of, step, len(sums), params.ndim),
        in_specs=[pl.BlockSpec(memory_space=pltpu.SMEM)] + [vmem] * len(operands),
        out_specs=[vmem] * len(out_shape),
        out_shape=out_shape,
        compiler_params=pltpu.CompilerParams(vmem_limit_bytes=4 * 1024 * 1024),
        cost_estimate=pl.CostEstimate(flops=10000, bytes_accessed=100000, transcendentals=0),
        name=f"{name}_{step}",
    )(rate, *operands)
    if not step:
        return params, [], outs[0]
    if step < ADAM_STEPS:
        return outs[0], outs[1:3], outs[3]
    return outs[0], [], None


def pixel_constants(n_tiles, blocks):
    pixel = np.arange(n_tiles * LANES).reshape(n_tiles, LANES)
    line = pixel // IMG_WIDTH
    across = (pixel % IMG_WIDTH).astype(np.float32) - np.float32((IMG_WIDTH - 1) / 2.0)
    downward = (line + (IMG_HEIGHT - WIN_ROWS) // 2).astype(np.float32) - np.float32(
        (IMG_HEIGHT - 1) / 2.0
    )
    ray = np.stack([across, downward]).reshape(2, blocks, n_tiles // blocks, LANES)
    first = line[:, 0]
    base = (line != first[:, None]).astype(np.int32) * TABLE_PAIRS
    lines = np.stack([first, np.minimum(first + 1, WIN_ROWS - 1)])
    pick = (lines[:, :, None] == np.arange(WIN_ROWS)).astype(np.float32)
    return jnp.asarray(base), jnp.asarray(ray), pick


def tree_sum(parts):
    while len(parts) > 1:
        parts = [a + b for a, b in zip(parts[::2], parts[1::2])]
    return parts[0]


def xor_permute(value, axis, bit, size):
    return lax.ppermute(value, axis, [(c, c ^ bit) for c in range(size)])


def fast_body(n_row, n_col, pointmaps, confidence, valid_blocks, log_depth, camera, pair_pose, step_sizes):
    rows, cols = pointmaps.shape[:2]
    pixels = pointmaps.shape[4]
    n_tiles = pixels // LANES
    tile = n_tiles // n_col
    sizes = (rows, cols, n_col, n_row, tile)
    row_index = lax.axis_index("row")
    col_index = lax.axis_index("col")
    core = col_index % 2
    me = jnp.stack([row_index, col_index]).astype(jnp.int32)
    f32 = jnp.float32

    x = pointmaps.transpose(0, 1, 3, 2, 4).reshape(rows, cols, 3, 2, n_tiles, LANES)
    x = x.transpose(0, 1, 2, 4, 3, 5).reshape(rows, cols, 3, 2 * n_tiles, LANES)
    conf = confidence.reshape(rows, cols, 2, n_tiles, LANES)
    conf = conf.transpose(0, 1, 3, 2, 4).reshape(rows, cols, 2 * n_tiles, LANES)

    base, ray, pick = pixel_constants(n_tiles, n_col)
    first_ids = row_index * rows + jnp.arange(rows, dtype=jnp.int32)
    second_ids = col_index * cols + jnp.arange(cols, dtype=jnp.int32)
    different = (first_ids[:, None] != second_ids[None, :]).astype(f32)
    share = different / (2.0 * (IMAGES - 1))
    valid = (valid_blocks.astype(f32)).reshape(rows * cols, WIN_ROWS)
    picked = lax.dot_general(
        jnp.asarray(pick.reshape(-1, WIN_ROWS)), valid, (((1,), (1,)), ((), ()))
    )
    picked = picked * share.reshape(1, rows * cols)
    picked = picked.reshape(2, n_tiles, rows * cols // TABLE_PAIRS, TABLE_PAIRS)
    table = picked.transpose(2, 1, 0, 3).reshape(-1, n_tiles, 2 * TABLE_PAIRS)

    def relative(value):
        return jnp.where(core == 0, value, value[::-1])

    def swap_perm(m):
        pairs = []
        for r in range(n_row):
            for c in range(n_col):
                to = (c // 2) * n_col + 2 * r + (m ^ (c & 1))
                pairs.append((r * n_col + c, to))
        return pairs

    def exchange(value, m):
        return lax.ppermute(value, ("row", "col"), swap_perm(m))

    def spread(row_part, col_part):
        own, other, down = [row_part], [], [col_part]
        for d in range(1, n_col // 2):
            own.append(xor_permute(row_part, "col", 2 * d, n_col))
        for e in range(1, n_row):
            down.append(xor_permute(col_part, "row", e, n_row))
        for d in range(n_col // 2):
            other.append(xor_permute(own[d], "col", 1, n_col))
        flat = []
        for d in range(n_col // 2):
            flat += [own[d], other[d]]
        return flat + down

    block = 2 * tile * SUBLANES

    def reduce_blocks(keep, send, cam, col_parts):
        got = xor_permute(send, "col", 1, n_col)
        cam = cam + xor_permute(cam, "col", 1, n_col)
        total = (keep + got).reshape(n_col // 2, block, LANES)
        col_total = col_parts[0]
        for e in range(1, n_row):
            col_total = col_total + xor_permute(col_parts[e], "row", e, n_row)
        row_total, cams = total[0], [cam]
        for d in range(1, n_col // 2):
            message = jnp.concatenate([total[d], cam], axis=0)
            message = xor_permute(message, "col", 2 * d, n_col)
            row_total = row_total + message[:block]
            cams.append(message[block:])
        cam_total = tree_sum(cams)
        row_total = row_total.reshape(2, tile, SUBLANES, LANES)
        col_total = col_total.reshape(2, tile, SUBLANES, LANES)
        return row_total, col_total, cam_total

    depth = log_depth.reshape(2, SUBLANES, tile, LANES).transpose(0, 2, 1, 3)
    depth = relative(depth)
    col_depth = jnp.stack([exchange(depth[m], m) for m in range(2)])
    depths = spread(depth.reshape(-1, LANES), col_depth.reshape(-1, LANES))

    rates = [step_sizes[k : k + 1] for k in range(3)]
    camera_now, camera_state, camera_coef = update(
        camera_grads, 0, rates[1], camera.T, [], [], "cameras"
    )
    pair_now, pair_state, pair_coef = update(
        pair_grads, 0, rates[2], pair_pose.transpose(1, 2, 0), [], [], "pairs"
    )
    totals = None
    block_totals = []
    for step in range(1, ADAM_STEPS + 1):
        outs = grads_of_pairs(
            step,
            sizes,
            me,
            pair_coef,
            camera_coef,
            step_sizes,
            x,
            conf,
            table,
            (base, ray),
            depths,
            totals,
        )
        keep, send = outs[:2]
        col_parts = outs[2 : 2 + n_row]
        pair_sums, cam_sums = outs[2 + n_row :]
        row_total, col_total, cam_sums = reduce_blocks(keep, send, cam_sums, col_parts)
        if step < ADAM_STEPS:
            received = [
                exchange(jnp.stack([row_total[m], col_total[m]]), m) for m in range(2)
            ]
            total = row_total + jnp.stack([v[1] for v in received])
            col_total = col_total + jnp.stack([v[0] for v in received])
            message = jnp.concatenate([col_total.reshape(-1, LANES), cam_sums], axis=0)
            totals = spread(total.reshape(-1, LANES), message)
            cam_parts = totals[n_col:]
        else:
            received = [exchange(col_total[m], m) for m in range(2)]
            total = row_total + jnp.stack(received)
            others = [xor_permute(cam_sums, "row", e, n_row) for e in range(1, n_row)]
            cam_parts = [cam_sums, *others]
        block_totals.append(total)
        camera_now, camera_state, camera_coef = update(
            camera_grads, step, rates[1], camera_now, cam_parts, camera_state, "cameras"
        )
        pair_sums = jnp.sum(pair_sums, axis=-1).transpose(1, 2, 0)
        pair_now, pair_state, pair_coef = update(
            pair_grads, step, rates[2], pair_now, [pair_sums], pair_state, "pairs"
        )

    depth_now = depth
    depth_state = (jnp.zeros_like(depth),) * 2
    for step in range(1, ADAM_STEPS + 1):
        depth_now, *depth_state = adam_step(
            depth_now, block_totals[step - 1], *depth_state, step, step_sizes[0]
        )
    depth_now = relative(depth_now).transpose(0, 2, 1, 3).reshape(log_depth.shape)
    return depth_now, camera_now.T, pair_now.transpose(2, 0, 1)


def solution(mesh):
    n_row, n_col = mesh.shape["row"], mesh.shape["col"]
    in_specs = (
        P("row", "col", None, None, None),
        P("row", "col", None, None),
        P("row", "col", None),
        P("row", "col"),
        P(),
        P("row", "col", None),
        P(),
    )
    out_specs = (P("row", "col"), P(), P("row", "col", None))

    def body(pointmaps, *rest):
        rows, cols, pixels = pointmaps.shape[0], pointmaps.shape[1], pointmaps.shape[4]
        whole_tiles = pixels % (LANES * n_col) == 0 and (pixels // LANES) % SUBLANES == 0
        whole_tables = (rows * cols) % TABLE_PAIRS == 0
        paired = IMAGES <= LANES and rows == 2 * SUBLANES and cols == SUBLANES and n_col == 2 * n_row
        power = n_row & (n_row - 1) == 0
        if whole_tiles and whole_tables and paired and power:
            return fast_body(n_row, n_col, pointmaps, *rest)
        return general_body(pointmaps, *rest)

    return jax.shard_map(body, mesh=mesh, in_specs=in_specs, out_specs=out_specs, check_vma=False)
```

```python
import functools

import numpy as np

import jax
import jax.numpy as jnp
from jax import lax
from jax.experimental import pallas as pl
from jax.experimental.pallas import tpu as pltpu
from jax.sharding import PartitionSpec as P

IMAGES = 64
IMG_WIDTH = 224
IMG_HEIGHT = 224
WIN_ROWS = 64
ADAM_STEPS = 2

BETA_ONE = 0.9
BETA_TWO = 0.999
ADAM_EPS = 0.001
SOFTEN = 0.01

LANES = 128
SUBLANES = 8
TABLE_PAIRS = 64


def rotation(quaternion):
    length = jnp.sqrt(jnp.sum(quaternion * quaternion, axis=-1))
    w = quaternion[..., 0] / length
    x = quaternion[..., 1] / length
    y = quaternion[..., 2] / length
    z = quaternion[..., 3] / length
    return [
        [1.0 - 2.0 * (y * y + z * z), 2.0 * (x * y - w * z), 2.0 * (x * z + w * y)],
        [2.0 * (x * y + w * z), 1.0 - 2.0 * (x * x + z * z), 2.0 * (y * z - w * x)],
        [2.0 * (x * z - w * y), 2.0 * (y * z + w * x), 1.0 - 2.0 * (x * x + y * y)],
    ]


def adam_step(param, grad, first, second, step_number, step_size):
    first = BETA_ONE * first + (1.0 - BETA_ONE) * grad
    second = BETA_TWO * second + (1.0 - BETA_TWO) * grad * grad
    update = (
        step_size
        * (first / (1.0 - BETA_ONE**step_number))
        / (jnp.sqrt(second / (1.0 - BETA_TWO**step_number)) + ADAM_EPS)
    )
    return (param - update, first, second)


def world_points(log_depths, cameras):
    pixel_count = log_depths.shape[-1]
    position = jnp.arange(pixel_count, dtype=jnp.int32)
    across = (position % IMG_WIDTH).astype(jnp.float32) - (IMG_WIDTH - 1) / 2.0
    downward = (position // IMG_WIDTH + (IMG_HEIGHT - WIN_ROWS) // 2).astype(jnp.float32) - (
        IMG_HEIGHT - 1
    ) / 2.0
    focal_len = jnp.exp(cameras[:, 7:8])
    depth_map = jnp.exp(log_depths)
    ray_parts = (
        across[None, :] / focal_len * depth_map,
        downward[None, :] / focal_len * depth_map,
        depth_map,
    )
    turned = rotation(cameras[:, 0:4])
    return [
        turned[k][0][:, None] * ray_parts[0]
        + turned[k][1][:, None] * ray_parts[1]
        + turned[k][2][:, None] * ray_parts[2]
        + cameras[:, 4 + k][:, None]
        for k in range(3)
    ]


def pair_loss(
    first_depth,
    second_depth,
    first_camera,
    second_camera,
    pair_params,
    pointmaps,
    confidence,
    valid_blocks,
    first_ids,
    second_ids,
):
    first_world = world_points(first_depth, first_camera)
    second_world = world_points(second_depth, second_camera)
    pair_rotation = rotation(pair_params[..., 0:4])
    pair_scale = jnp.exp(pair_params[..., 7])
    pair_keep = (first_ids[:, None] != second_ids[None, :]).astype(jnp.float32)
    pixel_keep = (
        jnp.repeat(valid_blocks.astype(jnp.float32), IMG_WIDTH, axis=2) * pair_keep[:, :, None]
    )
    loss_sum = jnp.zeros((), jnp.float32)
    for side_index in range(2):
        if side_index == 0:
            points_side = [first_world[k][:, None, :] for k in range(3)]
        else:
            points_side = [second_world[k][None, :, :] for k in range(3)]
        source = [pointmaps[:, :, side_index, k, :].astype(jnp.float32) for k in range(3)]
        squared = SOFTEN
        for k in range(3):
            aligned = (
                pair_scale[..., None]
                * (
                    pair_rotation[k][0][..., None] * source[0]
                    + pair_rotation[k][1][..., None] * source[1]
                    + pair_rotation[k][2][..., None] * source[2]
                )
                + pair_params[..., 4 + k][..., None]
            )
            residual = points_side[k] - aligned
            squared = squared + residual * residual
        weight = confidence[:, :, side_index, :].astype(jnp.float32) * pixel_keep
        loss_sum = loss_sum + jnp.sum(weight * jnp.sqrt(squared))
    return loss_sum / (2.0 * (IMAGES - 1))


def general_body(pointmaps, confidence, valid_blocks, log_depth, camera, pair_pose, step_sizes):
    row_count = pointmaps.shape[0]
    col_count = pointmaps.shape[1]
    row_index = lax.axis_index("row")
    col_index = lax.axis_index("col")
    first_ids = row_index * row_count + jnp.arange(row_count, dtype=jnp.int32)
    second_ids = col_index * col_count + jnp.arange(col_count, dtype=jnp.int32)

    def local_loss(row_depth, col_depth, cameras, pair_params):
        first_camera = lax.dynamic_slice_in_dim(cameras, row_index * row_count, row_count, 0)
        second_camera = lax.dynamic_slice_in_dim(cameras, col_index * col_count, col_count, 0)
        return pair_loss(
            row_depth,
            col_depth,
            first_camera,
            second_camera,
            pair_params,
            pointmaps,
            confidence,
            valid_blocks,
            first_ids,
            second_ids,
        )

    depth_now, camera_now, pair_now = (log_depth, camera, pair_pose)
    depth_first = jnp.zeros_like(log_depth)
    depth_second = jnp.zeros_like(log_depth)
    camera_first = jnp.zeros_like(camera)
    camera_second = jnp.zeros_like(camera)
    pair_first = jnp.zeros_like(pair_pose)
    pair_second = jnp.zeros_like(pair_pose)
    for step_number in range(1, ADAM_STEPS + 1):
        row_depth = lax.all_gather(depth_now, "col", axis=1, tiled=True)
        every_image = lax.all_gather(depth_now, "row", axis=0, tiled=True)
        col_depth = lax.all_to_all(every_image, "col", split_axis=0, concat_axis=1, tiled=True)
        row_grad, col_grad, cam_grad, pair_grad = jax.grad(local_loss, argnums=(0, 1, 2, 3))(
            row_depth, col_depth, camera_now, pair_now
        )
        returned = lax.all_to_all(col_grad, "col", split_axis=1, concat_axis=0, tiled=True)
        from_cols = lax.psum_scatter(returned, "row", scatter_dimension=0, tiled=True)
        depth_grad = lax.psum_scatter(row_grad, "col", scatter_dimension=1, tiled=True)
        depth_grad = depth_grad + from_cols
        cam_total = lax.psum(cam_grad, ("row", "col"))
        depth_now, depth_first, depth_second = adam_step(
            depth_now, depth_grad, depth_first, depth_second, step_number, step_sizes[0]
        )
        camera_now, camera_first, camera_second = adam_step(
            camera_now, cam_total, camera_first, camera_second, step_number, step_sizes[1]
        )
        pair_now, pair_first, pair_second = adam_step(
            pair_now, pair_grad, pair_first, pair_second, step_number, step_sizes[2]
        )
    return (depth_now, camera_now, pair_now)


def pick_lanes(values, index):
    numbers = lax.GatherDimensionNumbers(
        offset_dims=(),
        collapsed_slice_dims=(1,),
        start_index_map=(1,),
        operand_batching_dims=(0,),
        start_indices_batching_dims=(0,),
    )
    return lax.gather(
        values,
        index[..., None],
        numbers,
        slice_sizes=(1, 1),
        mode=lax.GatherScatterMode.PROMISE_IN_BOUNDS,
    )


def cross(a, b):
    return [
        a[1] * b[2] - a[2] * b[1],
        a[2] * b[0] - a[0] * b[2],
        a[0] * b[1] - a[1] * b[0],
    ]


def grad_kernel(shape, step, *refs):
    rows, cols, slots, row_slots, tile = shape
    n_dep = slots + row_slots
    refs = list(refs)
    me, pair, cam, rate, x_ref, conf_ref, table, lane_base, ray = refs[:9]
    depth_refs = refs[9 : 9 + n_dep]
    at = 9 + n_dep
    grad_refs = None
    if step > 1:
        grad_refs = refs[at : at + n_dep]
        at += n_dep
    keep_out, send_out = refs[at : at + 2]
    col_out = refs[at + 2 : at + 2 + row_slots]
    at += 2 + row_slots
    pair_out, cam_out = refs[at : at + 2]
    chi_i, chi_j, grad_i, grad_j, wide = refs[at + 2 :]

    i = pl.program_id(0)
    my_row, my_col = me[0], me[1]
    core = my_col & 1
    n_tiles = chi_i.shape[1]

    def depth_of(slot, start):
        take = pl.ds(start, tile, stride=SUBLANES)
        value = depth_refs[slot][take, :]
        if step > 1:
            g = grad_refs[slot][take, :]
            value = value - rate[0] * g / (jnp.abs(g) + ADAM_EPS)
        return jnp.exp(value)

    def put_points(dst, image, slot, start, block):
        depth = depth_of(slot, start)
        across = ray[0, block] / cam[12, image] * depth
        downward = ray[1, block] / cam[12, image] * depth
        for k in range(3):
            value = (
                cam[3 * k, image] * across
                + cam[3 * k + 1, image] * downward
                + cam[3 * k + 2, image] * depth
                + cam[9 + k, image]
            )
            dst[k, pl.ds(block * tile, tile), :] = value

    def finish(points, grads, image, block, sums):
        take = pl.ds(block * tile, tile)
        g = [grads[k, take, :] for k in range(3)]
        v = [points[k, take, :] - cam[9 + k, image] for k in range(3)]
        axis = [cam[3 * k + 2, image] for k in range(3)]
        by_depth = g[0] * v[0] + g[1] * v[1] + g[2] * v[2]
        depth = axis[0] * v[0] + axis[1] * v[1] + axis[2] * v[2]
        along = axis[0] * g[0] + axis[1] * g[1] + axis[2] * g[2]
        new = g + cross(v, g) + [by_depth - depth * along]
        return by_depth, [s + n for s, n in zip(sums, new)]

    def stack_sums(sums):
        parts = [jnp.sum(s, axis=0, keepdims=True) for s in sums]
        return jnp.concatenate(parts + [jnp.zeros((1, LANES), jnp.float32)], axis=0)

    def add_camera(image, sums):
        total = jnp.sum(stack_sums(sums), axis=1, keepdims=True)
        lane = lax.broadcasted_iota(jnp.int32, (SUBLANES, LANES), 1)
        cam_out[...] += jnp.where(lane == image, total, 0.0)

    def col_block(e, k_slot):
        return (my_row ^ e) * 2 + (k_slot ^ core)

    @pl.when(i == 0)
    def _():
        def one(j, carry):
            for e in range(row_slots):
                for k_slot in range(2):
                    put_points(
                        chi_j.at[j],
                        my_col * cols + j,
                        slots + e,
                        k_slot * tile * SUBLANES + j,
                        col_block(e, k_slot),
                    )
            return carry

        lax.fori_loop(0, cols, one, 0)
        grad_j[...] = jnp.zeros_like(grad_j)
        cam_out[...] = jnp.zeros_like(cam_out)

    t, m = i // SUBLANES, i % SUBLANES
    for d in range(slots):
        block = my_col ^ d
        t_slot = t ^ core ^ (d & 1)
        put_points(
            chi_i, my_row * rows + i, d, t_slot * tile * SUBLANES + m, block
        )
    grad_i[...] = jnp.zeros_like(grad_i)

    both = 2 * SUBLANES

    def one_pair(j, carry):
        q = i * cols + j
        shift = [pair[j, 9 + k, i] for k in range(3)]
        scale = pair[j, 12, i]
        which = q // TABLE_PAIRS
        lane_at = q % TABLE_PAIRS
        turn = [pair[j, n, i] for n in range(9)]

        def one_chunk(ch, sums):
            packed = pl.ds(pl.multiple_of(ch * both, both), both)
            take = pl.ds(pl.multiple_of(ch * SUBLANES, SUBLANES), SUBLANES)
            for k in range(3):
                wide[k, packed, :] = x_ref[0, j, k, packed, :].astype(jnp.float32)
            wide[3, packed, :] = conf_ref[0, j, packed, :].astype(jnp.float32)
            keep = pick_lanes(table[which, take, :], lane_base[take, :] + lane_at)
            for side, points, grads in ((0, chi_i, grad_i), (1, chi_j.at[j], grad_j.at[j])):
                alternate = pl.ds(ch * both + side, SUBLANES, stride=2)
                x = [wide[k, alternate, :] for k in range(3)]
                weight = wide[3, alternate, :] * keep
                y, r = [], []
                squared = SOFTEN
                for k in range(3):
                    y.append(
                        turn[3 * k] * x[0] + turn[3 * k + 1] * x[1] + turn[3 * k + 2] * x[2]
                    )
                    r.append(points[k, take, :] - (scale * y[k] + shift[k]))
                    squared = squared + r[k] * r[k]
                scaled = weight * lax.rsqrt(squared)
                g = [scaled * r[k] for k in range(3)]
                for k in range(3):
                    grads[k, take, :] += g[k]
                trace = g[0] * y[0] + g[1] * y[1] + g[2] * y[2]
                new = g + cross(g, y) + [trace]
                sums = tuple(s + n for s, n in zip(sums, new))
            return sums

        zero = jnp.zeros((SUBLANES, LANES), jnp.float32)
        sums = lax.fori_loop(0, n_tiles // SUBLANES, one_chunk, (zero,) * 7, unroll=True)
        pair_out[0, j] = stack_sums(sums)
        return carry

    lax.fori_loop(0, cols, one_pair, 0)

    zero = jnp.zeros((tile, LANES), jnp.float32)
    sums = [zero] * 7
    for d in range(slots):
        block = my_col ^ d
        t_slot = t ^ core ^ (d & 1)
        value, sums = finish(chi_i, grad_i, my_row * rows + i, block, sums)
        out = send_out if d & 1 else keep_out
        start = (d // 2) * (2 * tile * SUBLANES) + t_slot * tile * SUBLANES + m
        out[pl.ds(start, tile, stride=SUBLANES), :] = value
    add_camera(my_row * rows + i, sums)

    @pl.when(i == rows - 1)
    def _():
        def one(j, carry):
            sums = [zero] * 7
            for e in range(row_slots):
                for k_slot in range(2):
                    value, sums = finish(
                        chi_j.at[j], grad_j.at[j], my_col * cols + j, col_block(e, k_slot), sums
                    )
                    start = k_slot * tile * SUBLANES + j
                    col_out[e][pl.ds(start, tile, stride=SUBLANES), :] = value
            add_camera(my_col * cols + j, sums)
            return carry

        lax.fori_loop(0, cols, one, 0)


def grads_of_pairs(step, sizes, me, pair, cam, rate, x, conf, table, consts, depths, totals):
    rows, cols, slots, row_slots, tile = sizes
    n_rows = 2 * slots * tile
    smem = pl.BlockSpec(memory_space=pltpu.SMEM)
    vmem = pl.BlockSpec(memory_space=pltpu.VMEM)
    operands = [me, pair, cam, rate, x, conf, table, *consts, *depths]
    if step > 1:
        operands += totals
    in_specs = [smem] * 4 + [
        pl.BlockSpec((1, cols, 3, n_rows, LANES), lambda i: (i, 0, 0, 0, 0)),
        pl.BlockSpec((1, cols, n_rows, LANES), lambda i: (i, 0, 0, 0)),
    ]
    in_specs += [vmem] * (len(operands) - len(in_specs))
    block = 2 * tile * SUBLANES
    f32 = jnp.float32
    out_shape = [
        jax.ShapeDtypeStruct((slots // 2 * block, LANES), f32),
        jax.ShapeDtypeStruct((slots // 2 * block, LANES), f32),
        *[jax.ShapeDtypeStruct((block, LANES), f32)] * row_slots,
        jax.ShapeDtypeStruct((rows, cols, SUBLANES, LANES), f32),
        jax.ShapeDtypeStruct((SUBLANES, LANES), f32),
    ]
    out_specs = [vmem] * (2 + row_slots) + [
        pl.BlockSpec((1, cols, SUBLANES, LANES), lambda i: (i, 0, 0, 0)),
        vmem,
    ]
    work = rows * cols * 3 * n_rows * LANES
    return pl.pallas_call(
        functools.partial(grad_kernel, sizes, step),
        grid=(rows,),
        in_specs=in_specs,
        out_specs=out_specs,
        out_shape=out_shape,
        scratch_shapes=[
            pltpu.VMEM((3, n_rows // 2, LANES), f32),
            pltpu.VMEM((cols, 3, n_rows // 2, LANES), f32),
            pltpu.VMEM((3, n_rows // 2, LANES), f32),
            pltpu.VMEM((cols, 3, n_rows // 2, LANES), f32),
            pltpu.VMEM((4, n_rows, LANES), f32),
        ],
        compiler_params=pltpu.CompilerParams(
            dimension_semantics=("arbitrary",), vmem_limit_bytes=52 * 1024 * 1024
        ),
        cost_estimate=pl.CostEstimate(
            flops=20 * work, bytes_accessed=3 * work, transcendentals=work // 3
        ),
    )(*operands)


def rotation_of(q):
    length = jnp.sqrt(q[0] * q[0] + q[1] * q[1] + q[2] * q[2] + q[3] * q[3])
    w, x, y, z = (part / length for part in q)
    return [
        1.0 - 2.0 * (y * y + z * z),
        2.0 * (x * y - w * z),
        2.0 * (x * z + w * y),
        2.0 * (x * y + w * z),
        1.0 - 2.0 * (x * x + z * z),
        2.0 * (y * z - w * x),
        2.0 * (x * z - w * y),
        2.0 * (y * z + w * x),
        1.0 - 2.0 * (x * x + y * y),
    ]


def quaternion_grad(q, torque):
    w, v = q[0], q[1:4]
    factor = 2.0 / (w * w + v[0] * v[0] + v[1] * v[1] + v[2] * v[2])
    c = cross(torque, v)
    real = -(torque[0] * v[0] + torque[1] * v[1] + torque[2] * v[2])
    return [factor * real] + [factor * (w * torque[k] + c[k]) for k in range(3)]


def pair_grads(p, s):
    scale = jnp.exp(p[7])
    parts = quaternion_grad(p, [scale * s[k] for k in (3, 4, 5)])
    return parts + [-s[0], -s[1], -s[2], -scale * s[6]]


def camera_grads(p, s):
    return quaternion_grad(p, s[3:6]) + [s[0], s[1], s[2], -s[6]]


def update_kernel(grads_of, step, n_sums, axes, *refs):
    refs = list(refs)
    rate, params = refs[:2]

    def at(ref, k):
        return ref.at[:, k, :] if axes == 3 else ref.at[pl.ds(k, 1), :]

    p = [at(params, k)[...] for k in range(8)]
    rest = refs[2:]
    if step:
        width = p[0].shape[-1]
        parts = []
        for sums in rest[:n_sums]:
            top = sums.shape[-2] - SUBLANES
            if axes == 3:
                parts.append([sums[:, k, :] for k in range(7)])
            else:
                parts.append([sums[pl.ds(top + k, 1), pl.ds(0, width)] for k in range(7)])
        total = [tree_sum([part[k] for part in parts]) for k in range(7)]
        g = grads_of(p, total)
        rest = rest[n_sums:]
        first, second = [jnp.zeros_like(v) for v in p], [jnp.zeros_like(v) for v in p]
        if step > 1:
            first = [at(rest[0], k)[...] for k in range(8)]
            second = [at(rest[1], k)[...] for k in range(8)]
            rest = rest[2:]
        for k in range(8):
            p[k], first[k], second[k] = adam_step(p[k], g[k], first[k], second[k], step, rate[0])
            at(rest[0], k)[...] = p[k]
            if step < ADAM_STEPS:
                at(rest[1], k)[...] = first[k]
                at(rest[2], k)[...] = second[k]
        rest = rest[3:] if step < ADAM_STEPS else rest[1:]
    if step < ADAM_STEPS:
        values = rotation_of(p[0:4]) + p[4:7] + [jnp.exp(p[7])]
        for k, value in enumerate(values):
            at(rest[0], k)[...] = value


def update(grads_of, step, rate, params, sums, state):
    f32 = jnp.float32
    like = jax.ShapeDtypeStruct(params.shape, f32)
    coef_shape = (*params.shape[:-2], 16, params.shape[-1])
    out_shape = []
    if step:
        out_shape += [like] * (3 if step < ADAM_STEPS else 1)
    if step < ADAM_STEPS:
        out_shape.append(jax.ShapeDtypeStruct(coef_shape, f32))
    vmem = pl.BlockSpec(memory_space=pltpu.VMEM)
    operands = [params, *sums, *(state if step > 1 else [])]
    outs = pl.pallas_call(
        functools.partial(update_kernel, grads_of, step, len(sums), params.ndim),
        in_specs=[pl.BlockSpec(memory_space=pltpu.SMEM)] + [vmem] * len(operands),
        out_specs=[vmem] * len(out_shape),
        out_shape=out_shape,
        compiler_params=pltpu.CompilerParams(vmem_limit_bytes=4 * 1024 * 1024),
        cost_estimate=pl.CostEstimate(flops=10000, bytes_accessed=100000, transcendentals=0),
    )
    outs = outs(rate, *operands)
    if not step:
        return params, [], outs[0]
    if step < ADAM_STEPS:
        return outs[0], outs[1:3], outs[3]
    return outs[0], [], None


def pixel_constants(n_tiles, blocks):
    pixel = np.arange(n_tiles * LANES).reshape(n_tiles, LANES)
    line = pixel // IMG_WIDTH
    across = (pixel % IMG_WIDTH).astype(np.float32) - np.float32((IMG_WIDTH - 1) / 2.0)
    downward = (line + (IMG_HEIGHT - WIN_ROWS) // 2).astype(np.float32) - np.float32(
        (IMG_HEIGHT - 1) / 2.0
    )
    ray = np.stack([across, downward]).reshape(2, blocks, n_tiles // blocks, LANES)
    first = line[:, 0]
    base = (line != first[:, None]).astype(np.int32) * TABLE_PAIRS
    lines = np.stack([first, np.minimum(first + 1, WIN_ROWS - 1)])
    pick = (lines[:, :, None] == np.arange(WIN_ROWS)).astype(np.float32)
    return jnp.asarray(base), jnp.asarray(ray), pick


def tree_sum(parts):
    while len(parts) > 1:
        parts = [a + b for a, b in zip(parts[::2], parts[1::2])]
    return parts[0]


def xor_permute(value, axis, bit, size):
    return lax.ppermute(value, axis, [(c, c ^ bit) for c in range(size)])


def fast_body(n_row, n_col, pointmaps, confidence, valid_blocks, log_depth, camera, pair_pose, step_sizes):
    rows, cols = pointmaps.shape[:2]
    pixels = pointmaps.shape[4]
    n_tiles = pixels // LANES
    tile = n_tiles // n_col
    sizes = (rows, cols, n_col, n_row, tile)
    row_index = lax.axis_index("row")
    col_index = lax.axis_index("col")
    core = col_index % 2
    me = jnp.stack([row_index, col_index]).astype(jnp.int32)
    f32 = jnp.float32

    x = pointmaps.transpose(0, 1, 3, 2, 4).reshape(rows, cols, 3, 2, n_tiles, LANES)
    x = x.transpose(0, 1, 2, 4, 3, 5).reshape(rows, cols, 3, 2 * n_tiles, LANES)
    conf = confidence.reshape(rows, cols, 2, n_tiles, LANES)
    conf = conf.transpose(0, 1, 3, 2, 4).reshape(rows, cols, 2 * n_tiles, LANES)

    base, ray, pick = pixel_constants(n_tiles, n_col)
    first_ids = row_index * rows + jnp.arange(rows, dtype=jnp.int32)
    second_ids = col_index * cols + jnp.arange(cols, dtype=jnp.int32)
    different = (first_ids[:, None] != second_ids[None, :]).astype(f32)
    share = different / (2.0 * (IMAGES - 1))
    valid = (valid_blocks.astype(f32)).reshape(rows * cols, WIN_ROWS)
    picked = lax.dot_general(
        jnp.asarray(pick.reshape(-1, WIN_ROWS)), valid, (((1,), (1,)), ((), ()))
    )
    picked = picked * share.reshape(1, rows * cols)
    picked = picked.reshape(2, n_tiles, rows * cols // TABLE_PAIRS, TABLE_PAIRS)
    table = picked.transpose(2, 1, 0, 3).reshape(-1, n_tiles, 2 * TABLE_PAIRS)

    def relative(value):
        return jnp.where(core == 0, value, value[::-1])

    def swap_perm(m):
        pairs = []
        for r in range(n_row):
            for c in range(n_col):
                to = (c // 2) * n_col + 2 * r + (m ^ (c & 1))
                pairs.append((r * n_col + c, to))
        return pairs

    def exchange(value, m):
        return lax.ppermute(value, ("row", "col"), swap_perm(m))

    def spread(row_part, col_part):
        own, other, down = [row_part], [], [col_part]
        for d in range(1, n_col // 2):
            own.append(xor_permute(row_part, "col", 2 * d, n_col))
        for e in range(1, n_row):
            down.append(xor_permute(col_part, "row", e, n_row))
        for d in range(n_col // 2):
            other.append(xor_permute(own[d], "col", 1, n_col))
        flat = []
        for d in range(n_col // 2):
            flat += [own[d], other[d]]
        return flat + down

    block = 2 * tile * SUBLANES

    def reduce_blocks(keep, send, cam, col_parts):
        got = xor_permute(send, "col", 1, n_col)
        cam = cam + xor_permute(cam, "col", 1, n_col)
        total = (keep + got).reshape(n_col // 2, block, LANES)
        col_total = col_parts[0]
        for e in range(1, n_row):
            col_total = col_total + xor_permute(col_parts[e], "row", e, n_row)
        row_total, cams = total[0], [cam]
        for d in range(1, n_col // 2):
            message = jnp.concatenate([total[d], cam], axis=0)
            message = xor_permute(message, "col", 2 * d, n_col)
            row_total = row_total + message[:block]
            cams.append(message[block:])
        cam_total = tree_sum(cams)
        row_total = row_total.reshape(2, tile, SUBLANES, LANES)
        col_total = col_total.reshape(2, tile, SUBLANES, LANES)
        return row_total, col_total, cam_total

    depth = log_depth.reshape(2, SUBLANES, tile, LANES).transpose(0, 2, 1, 3)
    depth = relative(depth)
    col_parts = [exchange(depth[m], m) for m in range(2)]
    col_depth = jnp.stack(col_parts)
    depths = spread(depth.reshape(-1, LANES), col_depth.reshape(-1, LANES))

    rates = [step_sizes[k : k + 1] for k in range(3)]
    camera_now, camera_state, camera_coef = update(camera_grads, 0, rates[1], camera.T, [], [])
    pair_now, pair_state, pair_coef = update(
        pair_grads, 0, rates[2], pair_pose.transpose(1, 2, 0), [], []
    )
    totals = None
    block_totals = []
    for step in range(1, ADAM_STEPS + 1):
        outs = grads_of_pairs(
            step,
            sizes,
            me,
            pair_coef,
            camera_coef,
            step_sizes,
            x,
            conf,
            table,
            (base, ray),
            depths,
            totals,
        )
        keep, send = outs[:2]
        col_parts = outs[2 : 2 + n_row]
        pair_sums, cam_sums = outs[2 + n_row :]
        row_total, col_total, cam_sums = reduce_blocks(keep, send, cam_sums, col_parts)
        if step < ADAM_STEPS:
            messages = [jnp.stack([row_total[m], col_total[m]]) for m in range(2)]
            received = [exchange(messages[m], m) for m in range(2)]
            total = row_total + jnp.stack([v[1] for v in received])
            col_total = col_total + jnp.stack([v[0] for v in received])
            message = jnp.concatenate([col_total.reshape(-1, LANES), cam_sums], axis=0)
            totals = spread(total.reshape(-1, LANES), message)
            cam_parts = totals[n_col:]
        else:
            received = [exchange(col_total[m], m) for m in range(2)]
            total = row_total + jnp.stack(received)
            others = [xor_permute(cam_sums, "row", e, n_row) for e in range(1, n_row)]
            cam_parts = [cam_sums, *others]
        block_totals.append(total)
        camera_now, camera_state, camera_coef = update(
            camera_grads, step, rates[1], camera_now, cam_parts, camera_state
        )
        pair_sums = jnp.sum(pair_sums, axis=-1).transpose(1, 2, 0)
        pair_now, pair_state, pair_coef = update(
            pair_grads, step, rates[2], pair_now, [pair_sums], pair_state
        )

    depth_now = depth
    depth_state = (jnp.zeros_like(depth),) * 2
    for step in range(1, ADAM_STEPS + 1):
        depth_now, *depth_state = adam_step(
            depth_now, block_totals[step - 1], *depth_state, step, step_sizes[0]
        )
    depth_now = relative(depth_now).transpose(0, 2, 1, 3).reshape(log_depth.shape)
    return depth_now, camera_now.T, pair_now.transpose(2, 0, 1)


def solution(mesh):
    n_row, n_col = mesh.shape["row"], mesh.shape["col"]
    in_specs = (
        P("row", "col", None, None, None),
        P("row", "col", None, None),
        P("row", "col", None),
        P("row", "col"),
        P(),
        P("row", "col", None),
        P(),
    )
    out_specs = (P("row", "col"), P(), P("row", "col", None))

    def body(pointmaps, *rest):
        rows, cols, pixels = pointmaps.shape[0], pointmaps.shape[1], pointmaps.shape[4]
        whole_tiles = pixels % (LANES * n_col) == 0 and (pixels // LANES) % SUBLANES == 0
        whole_tables = (rows * cols) % TABLE_PAIRS == 0
        paired = IMAGES <= LANES and rows == 2 * SUBLANES and cols == SUBLANES and n_col == 2 * n_row
        power = n_row & (n_row - 1) == 0
        if whole_tiles and whole_tables and paired and power:
            return fast_body(n_row, n_col, pointmaps, *rest)
        return general_body(pointmaps, *rest)

    return jax.shard_map(body, mesh=mesh, in_specs=in_specs, out_specs=out_specs, check_vma=False)
```

```python
import functools

import numpy as np

import jax
import jax.numpy as jnp
from jax import lax
from jax.experimental import pallas as pl
from jax.experimental.pallas import tpu as pltpu
from jax.sharding import PartitionSpec as P

IMAGES = 64
IMG_WIDTH = 224
IMG_HEIGHT = 224
WIN_ROWS = 64
ADAM_STEPS = 2

BETA_ONE = 0.9
BETA_TWO = 0.999
ADAM_EPS = 0.001
SOFTEN = 0.01

LANES = 128
SUBLANES = 8
TABLE_PAIRS = 64


def rotation(quaternion):
    length = jnp.sqrt(jnp.sum(quaternion * quaternion, axis=-1))
    w = quaternion[..., 0] / length
    x = quaternion[..., 1] / length
    y = quaternion[..., 2] / length
    z = quaternion[..., 3] / length
    return [
        [1.0 - 2.0 * (y * y + z * z), 2.0 * (x * y - w * z), 2.0 * (x * z + w * y)],
        [2.0 * (x * y + w * z), 1.0 - 2.0 * (x * x + z * z), 2.0 * (y * z - w * x)],
        [2.0 * (x * z - w * y), 2.0 * (y * z + w * x), 1.0 - 2.0 * (x * x + y * y)],
    ]


def adam_step(param, grad, first, second, step_number, step_size):
    first = BETA_ONE * first + (1.0 - BETA_ONE) * grad
    second = BETA_TWO * second + (1.0 - BETA_TWO) * grad * grad
    update = (
        step_size
        * (first / (1.0 - BETA_ONE**step_number))
        / (jnp.sqrt(second / (1.0 - BETA_TWO**step_number)) + ADAM_EPS)
    )
    return (param - update, first, second)


def world_points(log_depths, cameras):
    pixel_count = log_depths.shape[-1]
    position = jnp.arange(pixel_count, dtype=jnp.int32)
    across = (position % IMG_WIDTH).astype(jnp.float32) - (IMG_WIDTH - 1) / 2.0
    downward = (position // IMG_WIDTH + (IMG_HEIGHT - WIN_ROWS) // 2).astype(jnp.float32) - (
        IMG_HEIGHT - 1
    ) / 2.0
    focal_len = jnp.exp(cameras[:, 7:8])
    depth_map = jnp.exp(log_depths)
    ray_parts = (
        across[None, :] / focal_len * depth_map,
        downward[None, :] / focal_len * depth_map,
        depth_map,
    )
    turned = rotation(cameras[:, 0:4])
    return [
        turned[k][0][:, None] * ray_parts[0]
        + turned[k][1][:, None] * ray_parts[1]
        + turned[k][2][:, None] * ray_parts[2]
        + cameras[:, 4 + k][:, None]
        for k in range(3)
    ]


def pair_loss(
    first_depth,
    second_depth,
    first_camera,
    second_camera,
    pair_params,
    pointmaps,
    confidence,
    valid_blocks,
    first_ids,
    second_ids,
):
    first_world = world_points(first_depth, first_camera)
    second_world = world_points(second_depth, second_camera)
    pair_rotation = rotation(pair_params[..., 0:4])
    pair_scale = jnp.exp(pair_params[..., 7])
    pair_keep = (first_ids[:, None] != second_ids[None, :]).astype(jnp.float32)
    pixel_keep = (
        jnp.repeat(valid_blocks.astype(jnp.float32), IMG_WIDTH, axis=2) * pair_keep[:, :, None]
    )
    loss_sum = jnp.zeros((), jnp.float32)
    for side_index in range(2):
        if side_index == 0:
            points_side = [first_world[k][:, None, :] for k in range(3)]
        else:
            points_side = [second_world[k][None, :, :] for k in range(3)]
        source = [pointmaps[:, :, side_index, k, :].astype(jnp.float32) for k in range(3)]
        squared = SOFTEN
        for k in range(3):
            aligned = (
                pair_scale[..., None]
                * (
                    pair_rotation[k][0][..., None] * source[0]
                    + pair_rotation[k][1][..., None] * source[1]
                    + pair_rotation[k][2][..., None] * source[2]
                )
                + pair_params[..., 4 + k][..., None]
            )
            residual = points_side[k] - aligned
            squared = squared + residual * residual
        weight = confidence[:, :, side_index, :].astype(jnp.float32) * pixel_keep
        loss_sum = loss_sum + jnp.sum(weight * jnp.sqrt(squared))
    return loss_sum / (2.0 * (IMAGES - 1))


def general_body(pointmaps, confidence, valid_blocks, log_depth, camera, pair_pose, step_sizes):
    row_count = pointmaps.shape[0]
    col_count = pointmaps.shape[1]
    row_index = lax.axis_index("row")
    col_index = lax.axis_index("col")
    first_ids = row_index * row_count + jnp.arange(row_count, dtype=jnp.int32)
    second_ids = col_index * col_count + jnp.arange(col_count, dtype=jnp.int32)

    def local_loss(row_depth, col_depth, cameras, pair_params):
        first_camera = lax.dynamic_slice_in_dim(cameras, row_index * row_count, row_count, 0)
        second_camera = lax.dynamic_slice_in_dim(cameras, col_index * col_count, col_count, 0)
        return pair_loss(
            row_depth,
            col_depth,
            first_camera,
            second_camera,
            pair_params,
            pointmaps,
            confidence,
            valid_blocks,
            first_ids,
            second_ids,
        )

    depth_now, camera_now, pair_now = (log_depth, camera, pair_pose)
    depth_first = jnp.zeros_like(log_depth)
    depth_second = jnp.zeros_like(log_depth)
    camera_first = jnp.zeros_like(camera)
    camera_second = jnp.zeros_like(camera)
    pair_first = jnp.zeros_like(pair_pose)
    pair_second = jnp.zeros_like(pair_pose)
    for step_number in range(1, ADAM_STEPS + 1):
        row_depth = lax.all_gather(depth_now, "col", axis=1, tiled=True)
        every_image = lax.all_gather(depth_now, "row", axis=0, tiled=True)
        col_depth = lax.all_to_all(every_image, "col", split_axis=0, concat_axis=1, tiled=True)
        row_grad, col_grad, cam_grad, pair_grad = jax.grad(local_loss, argnums=(0, 1, 2, 3))(
            row_depth, col_depth, camera_now, pair_now
        )
        returned = lax.all_to_all(col_grad, "col", split_axis=1, concat_axis=0, tiled=True)
        from_cols = lax.psum_scatter(returned, "row", scatter_dimension=0, tiled=True)
        depth_grad = lax.psum_scatter(row_grad, "col", scatter_dimension=1, tiled=True)
        depth_grad = depth_grad + from_cols
        cam_total = lax.psum(cam_grad, ("row", "col"))
        depth_now, depth_first, depth_second = adam_step(
            depth_now, depth_grad, depth_first, depth_second, step_number, step_sizes[0]
        )
        camera_now, camera_first, camera_second = adam_step(
            camera_now, cam_total, camera_first, camera_second, step_number, step_sizes[1]
        )
        pair_now, pair_first, pair_second = adam_step(
            pair_now, pair_grad, pair_first, pair_second, step_number, step_sizes[2]
        )
    return (depth_now, camera_now, pair_now)


def pick_lanes(values, index):
    numbers = lax.GatherDimensionNumbers(
        offset_dims=(),
        collapsed_slice_dims=(1,),
        start_index_map=(1,),
        operand_batching_dims=(0,),
        start_indices_batching_dims=(0,),
    )
    return lax.gather(
        values,
        index[..., None],
        numbers,
        slice_sizes=(1, 1),
        mode=lax.GatherScatterMode.PROMISE_IN_BOUNDS,
    )


def cross(a, b):
    return [
        a[1] * b[2] - a[2] * b[1],
        a[2] * b[0] - a[0] * b[2],
        a[0] * b[1] - a[1] * b[0],
    ]


def grad_kernel(shape, step, *refs):
    rows, cols, slots, row_slots, tile = shape
    n_dep = slots + row_slots
    refs = list(refs)
    me, pair, cam, rate, x_ref, conf_ref, table, lane_base, ray = refs[:9]
    depth_refs = refs[9 : 9 + n_dep]
    at = 9 + n_dep
    grad_refs = None
    if step > 1:
        grad_refs = refs[at : at + n_dep]
        at += n_dep
    keep_out, send_out = refs[at : at + 2]
    col_out = refs[at + 2 : at + 2 + row_slots]
    at += 2 + row_slots
    pair_out, cam_out = refs[at : at + 2]
    chi_i, chi_j, grad_i, grad_j, wide = refs[at + 2 :]

    i = pl.program_id(0)
    my_row, my_col = me[0], me[1]
    core = my_col & 1
    n_tiles = chi_i.shape[1]

    def depth_of(slot, start):
        take = pl.ds(start, tile, stride=SUBLANES)
        value = depth_refs[slot][take, :]
        if step > 1:
            g = grad_refs[slot][take, :]
            value = value - rate[0] * g / (jnp.abs(g) + ADAM_EPS)
        return jnp.exp(value)

    def put_points(dst, image, slot, start, block):
        depth = depth_of(slot, start)
        across = ray[0, block] / cam[12, image] * depth
        downward = ray[1, block] / cam[12, image] * depth
        for k in range(3):
            value = (
                cam[3 * k, image] * across
                + cam[3 * k + 1, image] * downward
                + cam[3 * k + 2, image] * depth
                + cam[9 + k, image]
            )
            dst[k, pl.ds(block * tile, tile), :] = value

    def finish(points, grads, image, block, sums):
        take = pl.ds(block * tile, tile)
        g = [grads[k, take, :] for k in range(3)]
        v = [points[k, take, :] - cam[9 + k, image] for k in range(3)]
        axis = [cam[3 * k + 2, image] for k in range(3)]
        by_depth = g[0] * v[0] + g[1] * v[1] + g[2] * v[2]
        depth = axis[0] * v[0] + axis[1] * v[1] + axis[2] * v[2]
        along = axis[0] * g[0] + axis[1] * g[1] + axis[2] * g[2]
        new = g + cross(v, g) + [by_depth - depth * along]
        return by_depth, [s + n for s, n in zip(sums, new)]

    def stack_sums(sums):
        parts = [jnp.sum(s, axis=0, keepdims=True) for s in sums]
        return jnp.concatenate(parts + [jnp.zeros((1, LANES), jnp.float32)], axis=0)

    def add_camera(image, sums):
        total = jnp.sum(stack_sums(sums), axis=1, keepdims=True)
        lane = lax.broadcasted_iota(jnp.int32, (SUBLANES, LANES), 1)
        cam_out[...] += jnp.where(lane == image, total, 0.0)

    def col_block(e, k_slot):
        return (my_row ^ e) * 2 + (k_slot ^ core)

    @pl.when(i == 0)
    def _():
        def one(j, carry):
            for e in range(row_slots):
                for k_slot in range(2):
                    put_points(
                        chi_j.at[j],
                        my_col * cols + j,
                        slots + e,
                        k_slot * tile * SUBLANES + j,
                        col_block(e, k_slot),
                    )
            return carry

        lax.fori_loop(0, cols, one, 0)
        grad_j[...] = jnp.zeros_like(grad_j)
        cam_out[...] = jnp.zeros_like(cam_out)

    t, m = i // SUBLANES, i % SUBLANES
    for d in range(slots):
        block = my_col ^ d
        t_slot = t ^ core ^ (d & 1)
        put_points(
            chi_i, my_row * rows + i, d, t_slot * tile * SUBLANES + m, block
        )
    grad_i[...] = jnp.zeros_like(grad_i)

    both = 2 * SUBLANES

    def one_pair(j, carry):
        q = i * cols + j
        shift = [pair[j, 9 + k, i] for k in range(3)]
        scale = pair[j, 12, i]
        which = q // TABLE_PAIRS
        lane_at = q % TABLE_PAIRS
        turn = [pair[j, n, i] for n in range(9)]

        def one_chunk(ch, sums):
            packed = pl.ds(pl.multiple_of(ch * both, both), both)
            take = pl.ds(pl.multiple_of(ch * SUBLANES, SUBLANES), SUBLANES)
            for k in range(3):
                wide[k, packed, :] = x_ref[0, j, k, packed, :].astype(jnp.float32)
            wide[3, packed, :] = conf_ref[0, j, packed, :].astype(jnp.float32)
            keep = pick_lanes(table[which, take, :], lane_base[take, :] + lane_at)
            for side, points, grads in ((0, chi_i, grad_i), (1, chi_j.at[j], grad_j.at[j])):
                alternate = pl.ds(ch * both + side, SUBLANES, stride=2)
                x = [wide[k, alternate, :] for k in range(3)]
                weight = wide[3, alternate, :] * keep
                y, r = [], []
                squared = SOFTEN
                for k in range(3):
                    y.append(
                        turn[3 * k] * x[0] + turn[3 * k + 1] * x[1] + turn[3 * k + 2] * x[2]
                    )
                    r.append(points[k, take, :] - (scale * y[k] + shift[k]))
                    squared = squared + r[k] * r[k]
                scaled = weight * lax.rsqrt(squared)
                g = [scaled * r[k] for k in range(3)]
                for k in range(3):
                    grads[k, take, :] += g[k]
                trace = g[0] * y[0] + g[1] * y[1] + g[2] * y[2]
                new = g + cross(g, y) + [trace]
                sums = tuple(s + n for s, n in zip(sums, new))
            return sums

        zero = jnp.zeros((SUBLANES, LANES), jnp.float32)
        sums = lax.fori_loop(0, n_tiles // SUBLANES, one_chunk, (zero,) * 7, unroll=True)
        pair_out[0, j] = stack_sums(sums)
        return carry

    lax.fori_loop(0, cols, one_pair, 0)

    zero = jnp.zeros((tile, LANES), jnp.float32)
    sums = [zero] * 7
    for d in range(slots):
        block = my_col ^ d
        t_slot = t ^ core ^ (d & 1)
        value, sums = finish(chi_i, grad_i, my_row * rows + i, block, sums)
        out = send_out if d & 1 else keep_out
        start = (d // 2) * (2 * tile * SUBLANES) + t_slot * tile * SUBLANES + m
        out[pl.ds(start, tile, stride=SUBLANES), :] = value
    add_camera(my_row * rows + i, sums)

    @pl.when(i == rows - 1)
    def _():
        def one(j, carry):
            sums = [zero] * 7
            for e in range(row_slots):
                for k_slot in range(2):
                    value, sums = finish(
                        chi_j.at[j], grad_j.at[j], my_col * cols + j, col_block(e, k_slot), sums
                    )
                    start = k_slot * tile * SUBLANES + j
                    col_out[e][pl.ds(start, tile, stride=SUBLANES), :] = value
            add_camera(my_col * cols + j, sums)
            return carry

        lax.fori_loop(0, cols, one, 0)


def grads_of_pairs(step, sizes, me, pair, cam, rate, x, conf, table, consts, depths, totals):
    rows, cols, slots, row_slots, tile = sizes
    n_rows = 2 * slots * tile
    smem = pl.BlockSpec(memory_space=pltpu.SMEM)
    vmem = pl.BlockSpec(memory_space=pltpu.VMEM)
    operands = [me, pair, cam, rate, x, conf, table, *consts, *depths]
    if step > 1:
        operands += totals
    in_specs = [smem] * 4 + [
        pl.BlockSpec((1, cols, 3, n_rows, LANES), lambda i: (i, 0, 0, 0, 0)),
        pl.BlockSpec((1, cols, n_rows, LANES), lambda i: (i, 0, 0, 0)),
    ]
    in_specs += [vmem] * (len(operands) - len(in_specs))
    block = 2 * tile * SUBLANES
    f32 = jnp.float32
    out_shape = [
        jax.ShapeDtypeStruct((slots // 2 * block, LANES), f32),
        jax.ShapeDtypeStruct((slots // 2 * block, LANES), f32),
        *[jax.ShapeDtypeStruct((block, LANES), f32)] * row_slots,
        jax.ShapeDtypeStruct((rows, cols, SUBLANES, LANES), f32),
        jax.ShapeDtypeStruct((SUBLANES, LANES), f32),
    ]
    out_specs = [vmem] * (2 + row_slots) + [
        pl.BlockSpec((1, cols, SUBLANES, LANES), lambda i: (i, 0, 0, 0)),
        vmem,
    ]
    work = rows * cols * 3 * n_rows * LANES
    return pl.pallas_call(
        functools.partial(grad_kernel, sizes, step),
        grid=(rows,),
        in_specs=in_specs,
        out_specs=out_specs,
        out_shape=out_shape,
        scratch_shapes=[
            pltpu.VMEM((3, n_rows // 2, LANES), f32),
            pltpu.VMEM((cols, 3, n_rows // 2, LANES), f32),
            pltpu.VMEM((3, n_rows // 2, LANES), f32),
            pltpu.VMEM((cols, 3, n_rows // 2, LANES), f32),
            pltpu.VMEM((4, n_rows, LANES), f32),
        ],
        compiler_params=pltpu.CompilerParams(
            dimension_semantics=("arbitrary",), vmem_limit_bytes=52 * 1024 * 1024
        ),
        cost_estimate=pl.CostEstimate(
            flops=20 * work, bytes_accessed=3 * work, transcendentals=work // 3
        ),
    )(*operands)


def rotation_of(q):
    length = jnp.sqrt(q[0] * q[0] + q[1] * q[1] + q[2] * q[2] + q[3] * q[3])
    w, x, y, z = (part / length for part in q)
    return [
        1.0 - 2.0 * (y * y + z * z),
        2.0 * (x * y - w * z),
        2.0 * (x * z + w * y),
        2.0 * (x * y + w * z),
        1.0 - 2.0 * (x * x + z * z),
        2.0 * (y * z - w * x),
        2.0 * (x * z - w * y),
        2.0 * (y * z + w * x),
        1.0 - 2.0 * (x * x + y * y),
    ]


def quaternion_grad(q, torque):
    w, v = q[0], q[1:4]
    factor = 2.0 / (w * w + v[0] * v[0] + v[1] * v[1] + v[2] * v[2])
    c = cross(torque, v)
    real = -(torque[0] * v[0] + torque[1] * v[1] + torque[2] * v[2])
    return [factor * real] + [factor * (w * torque[k] + c[k]) for k in range(3)]


def pair_grads(p, s):
    scale = jnp.exp(p[7])
    parts = quaternion_grad(p, [scale * s[k] for k in (3, 4, 5)])
    return parts + [-s[0], -s[1], -s[2], -scale * s[6]]


def camera_grads(p, s):
    return quaternion_grad(p, s[3:6]) + [s[0], s[1], s[2], -s[6]]


def update_kernel(grads_of, step, n_sums, axes, *refs):
    refs = list(refs)
    rate, params = refs[:2]

    def at(ref, k):
        return ref.at[:, k, :] if axes == 3 else ref.at[pl.ds(k, 1), :]

    p = [at(params, k)[...] for k in range(8)]
    rest = refs[2:]
    if step:
        width = p[0].shape[-1]
        parts = []
        for sums in rest[:n_sums]:
            top = sums.shape[-2] - SUBLANES
            if axes == 3:
                parts.append([sums[:, k, :] for k in range(7)])
            else:
                parts.append([sums[pl.ds(top + k, 1), pl.ds(0, width)] for k in range(7)])
        total = [tree_sum([part[k] for part in parts]) for k in range(7)]
        g = grads_of(p, total)
        rest = rest[n_sums:]
        first, second = [jnp.zeros_like(v) for v in p], [jnp.zeros_like(v) for v in p]
        if step > 1:
            first = [at(rest[0], k)[...] for k in range(8)]
            second = [at(rest[1], k)[...] for k in range(8)]
            rest = rest[2:]
        for k in range(8):
            p[k], first[k], second[k] = adam_step(p[k], g[k], first[k], second[k], step, rate[0])
            at(rest[0], k)[...] = p[k]
            if step < ADAM_STEPS:
                at(rest[1], k)[...] = first[k]
                at(rest[2], k)[...] = second[k]
        rest = rest[3:] if step < ADAM_STEPS else rest[1:]
    if step < ADAM_STEPS:
        values = rotation_of(p[0:4]) + p[4:7] + [jnp.exp(p[7])]
        for k, value in enumerate(values):
            at(rest[0], k)[...] = value


def update(grads_of, step, rate, params, sums, state):
    f32 = jnp.float32
    like = jax.ShapeDtypeStruct(params.shape, f32)
    coef_shape = (*params.shape[:-2], 16, params.shape[-1])
    out_shape = []
    if step:
        out_shape += [like] * (3 if step < ADAM_STEPS else 1)
    if step < ADAM_STEPS:
        out_shape.append(jax.ShapeDtypeStruct(coef_shape, f32))
    vmem = pl.BlockSpec(memory_space=pltpu.VMEM)
    operands = [params, *sums, *(state if step > 1 else [])]
    outs = pl.pallas_call(
        functools.partial(update_kernel, grads_of, step, len(sums), params.ndim),
        in_specs=[pl.BlockSpec(memory_space=pltpu.SMEM)] + [vmem] * len(operands),
        out_specs=[vmem] * len(out_shape),
        out_shape=out_shape,
        compiler_params=pltpu.CompilerParams(vmem_limit_bytes=4 * 1024 * 1024),
        cost_estimate=pl.CostEstimate(flops=10000, bytes_accessed=100000, transcendentals=0),
    )
    outs = outs(rate, *operands)
    if not step:
        return params, [], outs[0]
    if step < ADAM_STEPS:
        return outs[0], outs[1:3], outs[3]
    return outs[0], [], None


def pixel_constants(n_tiles, blocks):
    pixel = np.arange(n_tiles * LANES).reshape(n_tiles, LANES)
    line = pixel // IMG_WIDTH
    across = (pixel % IMG_WIDTH).astype(np.float32) - np.float32((IMG_WIDTH - 1) / 2.0)
    downward = (line + (IMG_HEIGHT - WIN_ROWS) // 2).astype(np.float32) - np.float32(
        (IMG_HEIGHT - 1) / 2.0
    )
    ray = np.stack([across, downward]).reshape(2, blocks, n_tiles // blocks, LANES)
    first = line[:, 0]
    base = (line != first[:, None]).astype(np.int32) * TABLE_PAIRS
    lines = np.stack([first, np.minimum(first + 1, WIN_ROWS - 1)])
    pick = (lines[:, :, None] == np.arange(WIN_ROWS)).astype(np.float32)
    return jnp.asarray(base), jnp.asarray(ray), pick


def tree_sum(parts):
    while len(parts) > 1:
        parts = [a + b for a, b in zip(parts[::2], parts[1::2])]
    return parts[0]


def xor_permute(value, axis, bit, size):
    return lax.ppermute(value, axis, [(c, c ^ bit) for c in range(size)])


def fast_body(n_row, n_col, pointmaps, confidence, valid_blocks, log_depth, camera, pair_pose, step_sizes):
    rows, cols = pointmaps.shape[:2]
    pixels = pointmaps.shape[4]
    n_tiles = pixels // LANES
    tile = n_tiles // n_col
    sizes = (rows, cols, n_col, n_row, tile)
    row_index = lax.axis_index("row")
    col_index = lax.axis_index("col")
    core = col_index % 2
    me = jnp.stack([row_index, col_index]).astype(jnp.int32)
    f32 = jnp.float32

    x = pointmaps.transpose(0, 1, 3, 2, 4).reshape(rows, cols, 3, 2, n_tiles, LANES)
    x = x.transpose(0, 1, 2, 4, 3, 5).reshape(rows, cols, 3, 2 * n_tiles, LANES)
    conf = confidence.reshape(rows, cols, 2, n_tiles, LANES)
    conf = conf.transpose(0, 1, 3, 2, 4).reshape(rows, cols, 2 * n_tiles, LANES)

    base, ray, pick = pixel_constants(n_tiles, n_col)
    first_ids = row_index * rows + jnp.arange(rows, dtype=jnp.int32)
    second_ids = col_index * cols + jnp.arange(cols, dtype=jnp.int32)
    different = (first_ids[:, None] != second_ids[None, :]).astype(f32)
    share = different / (2.0 * (IMAGES - 1))
    valid = (valid_blocks.astype(f32)).reshape(rows * cols, WIN_ROWS)
    picked = lax.dot_general(
        jnp.asarray(pick.reshape(-1, WIN_ROWS)), valid, (((1,), (1,)), ((), ()))
    )
    picked = picked * share.reshape(1, rows * cols)
    picked = picked.reshape(2, n_tiles, rows * cols // TABLE_PAIRS, TABLE_PAIRS)
    table = picked.transpose(2, 1, 0, 3).reshape(-1, n_tiles, 2 * TABLE_PAIRS)

    def relative(value):
        return jnp.where(core == 0, value, value[::-1])

    def swap_perm(m):
        pairs = []
        for r in range(n_row):
            for c in range(n_col):
                to = (c // 2) * n_col + 2 * r + (m ^ (c & 1))
                pairs.append((r * n_col + c, to))
        return pairs

    def exchange(value, m):
        return lax.ppermute(value, ("row", "col"), swap_perm(m))

    def spread(row_part, col_part):
        own, other, down = [row_part], [], [col_part]
        for d in range(1, n_col // 2):
            own.append(xor_permute(row_part, "col", 2 * d, n_col))
        for e in range(1, n_row):
            down.append(xor_permute(col_part, "row", e, n_row))
        for d in range(n_col // 2):
            other.append(xor_permute(own[d], "col", 1, n_col))
        flat = []
        for d in range(n_col // 2):
            flat += [own[d], other[d]]
        return flat + down

    block = 2 * tile * SUBLANES

    def reduce_blocks(keep, send, cam, col_parts):
        got = xor_permute(send, "col", 1, n_col)
        cam = cam + xor_permute(cam, "col", 1, n_col)
        total = (keep + got).reshape(n_col // 2, block, LANES)
        col_total = col_parts[0]
        got = [xor_permute(col_parts[e], "row", e, n_row) for e in range(1, n_row)]
        for part in got:
            col_total = col_total + part
        row_total, cams = total[0], [cam]
        for d in range(1, n_col // 2):
            message = jnp.concatenate([total[d], cam], axis=0)
            message = xor_permute(message, "col", 2 * d, n_col)
            row_total = row_total + message[:block]
            cams.append(message[block:])
        cam_total = tree_sum(cams)
        row_total = row_total.reshape(2, tile, SUBLANES, LANES)
        col_total = col_total.reshape(2, tile, SUBLANES, LANES)
        return row_total, col_total, cam_total

    depth = log_depth.reshape(2, SUBLANES, tile, LANES).transpose(0, 2, 1, 3)
    depth = relative(depth)
    col_parts = [exchange(depth[m], m) for m in range(2)]
    col_depth = jnp.stack(col_parts)
    depths = spread(depth.reshape(-1, LANES), col_depth.reshape(-1, LANES))

    rates = [step_sizes[k : k + 1] for k in range(3)]
    camera_now, camera_state, camera_coef = update(camera_grads, 0, rates[1], camera.T, [], [])
    pair_now, pair_state, pair_coef = update(
        pair_grads, 0, rates[2], pair_pose.transpose(1, 2, 0), [], []
    )
    totals = None
    block_totals = []
    for step in range(1, ADAM_STEPS + 1):
        outs = grads_of_pairs(
            step,
            sizes,
            me,
            pair_coef,
            camera_coef,
            step_sizes,
            x,
            conf,
            table,
            (base, ray),
            depths,
            totals,
        )
        keep, send = outs[:2]
        col_parts = outs[2 : 2 + n_row]
        pair_sums, cam_sums = outs[2 + n_row :]
        row_total, col_total, cam_sums = reduce_blocks(keep, send, cam_sums, col_parts)
        if step < ADAM_STEPS:
            messages = [jnp.stack([row_total[m], col_total[m]]) for m in range(2)]
            received = [exchange(messages[m], m) for m in range(2)]
            total = row_total + jnp.stack([v[1] for v in received])
            col_total = col_total + jnp.stack([v[0] for v in received])
            message = jnp.concatenate([col_total.reshape(-1, LANES), cam_sums], axis=0)
            totals = spread(total.reshape(-1, LANES), message)
            cam_parts = totals[n_col:]
        else:
            received = [exchange(col_total[m], m) for m in range(2)]
            total = row_total + jnp.stack(received)
            others = [xor_permute(cam_sums, "row", e, n_row) for e in range(1, n_row)]
            cam_parts = [cam_sums, *others]
        block_totals.append(total)
        camera_now, camera_state, camera_coef = update(
            camera_grads, step, rates[1], camera_now, cam_parts, camera_state
        )
        pair_sums = jnp.sum(pair_sums, axis=-1).transpose(1, 2, 0)
        pair_now, pair_state, pair_coef = update(
            pair_grads, step, rates[2], pair_now, [pair_sums], pair_state
        )

    depth_now = depth
    depth_state = (jnp.zeros_like(depth),) * 2
    for step in range(1, ADAM_STEPS + 1):
        depth_now, *depth_state = adam_step(
            depth_now, block_totals[step - 1], *depth_state, step, step_sizes[0]
        )
    depth_now = relative(depth_now).transpose(0, 2, 1, 3).reshape(log_depth.shape)
    return depth_now, camera_now.T, pair_now.transpose(2, 0, 1)


def solution(mesh):
    n_row, n_col = mesh.shape["row"], mesh.shape["col"]
    in_specs = (
        P("row", "col", None, None, None),
        P("row", "col", None, None),
        P("row", "col", None),
        P("row", "col"),
        P(),
        P("row", "col", None),
        P(),
    )
    out_specs = (P("row", "col"), P(), P("row", "col", None))

    def body(pointmaps, *rest):
        rows, cols, pixels = pointmaps.shape[0], pointmaps.shape[1], pointmaps.shape[4]
        whole_tiles = pixels % (LANES * n_col) == 0 and (pixels // LANES) % SUBLANES == 0
        whole_tables = (rows * cols) % TABLE_PAIRS == 0
        paired = IMAGES <= LANES and rows == 2 * SUBLANES and cols == SUBLANES and n_col == 2 * n_row
        power = n_row & (n_row - 1) == 0
        if whole_tiles and whole_tables and paired and power:
            return fast_body(n_row, n_col, pointmaps, *rest)
        return general_body(pointmaps, *rest)

    return jax.shard_map(body, mesh=mesh, in_specs=in_specs, out_specs=out_specs, check_vma=False)
```
